32 devices in a mesh: grp: 4 (over z), leaf: 8 (over y, x, core).
Axes of the slice: x: 2, y: 2, z: 4, core: 2. Of those that a mesh axis runs over, the one named last changes fastest.
Arguments:
- basis_slab: bfloat16 [32768, 1024], P(('grp', 'leaf')), may hold values from -6 to 6
- live_counts: int32 [32], P(('grp', 'leaf')), may hold values from 128 to 1024, as said below
- pole_order: int32 [32, 1024], P(('grp', 'leaf')), may hold values from 0 to 1023, each once within a row
- leaf_diag: bfloat16 [32768, 1024], P(('grp', 'leaf')), may hold values from -0.1875 to 0.1875
- leaf_in: bfloat16 [32768, 128], P(('grp', 'leaf')), may hold values from -0.1875 to 0.1875
- leaf_out: bfloat16 [32768, 128], P(('grp', 'leaf')), may hold values from -0.5 to 0.5
- leaf_lift: bfloat16 [32, 128, 128], P(('grp', 'leaf')), may hold values from -0.375 to 0.375
- leaf_couple: bfloat16 [32, 128, 128], P(('grp', 'leaf')), may hold values from -0.5 to 0.5
- leaf_spread: bfloat16 [32, 128, 128], P(('grp', 'leaf')), may hold values from -0.4375 to 0.4375
- inner_lift: bfloat16 [28, 128, 128], replicated, may hold values from -0.375 to 0.375
- inner_couple: bfloat16 [30, 128, 128], replicated, may hold values from -0.5 to 0.5
- inner_spread: bfloat16 [28, 128, 128], replicated, may hold values from -0.4375 to 0.4375
Outputs:
- merged: bfloat16 [32768, 1024], P(('grp', 'leaf'))
The draws below stay inside these ranges and needn't reach their ends.
Inputs may be any that keep to these rules, and one draw needn't show every extreme that they name: `live_counts`: each count is 1024, 512, 256 or 128, and some leaf has 1024. `pole_order`: each row names every slot's pole once.
All inputs are finite; a program needn't handle non-finite values.
Results may differ from the reference program's by a relative error of at most 0.0055.
Values may be sent and summed in bfloat16 or wider, within the bound.
A program may use at most 64 MiB of HBM per device.

```python
import jax
import jax.numpy as jnp
from jax import lax

M = 1024
RANK = 128
R = 1024
N = 32768
N_GRP = 4
N_LEAF = 8
DEVICES = 32


def draw_live_counts(key, part):
    first_key, second_key = jax.random.split(jax.random.fold_in(key, 17))
    halvings = jax.random.randint(first_key, (N_GRP * N_LEAF,), 0, 4)
    counts = jnp.right_shift(jnp.full((N_GRP * N_LEAF,), M, jnp.int32), halvings.astype(jnp.int32))
    fullest = jax.random.randint(second_key, (), 0, N_GRP * N_LEAF)
    return counts.at[fullest].set(M).astype(jnp.int32)


def block_scale(key, dims, cuts, low, largest):
    gain = 1.0
    for axis_at, parts in cuts:
        draws = jax.random.uniform(jax.random.fold_in(jax.random.fold_in(key, 6), axis_at), (parts,), jnp.float32, low / len(cuts), largest / len(cuts))
        gain = gain * jnp.repeat(jnp.exp(draws), dims[axis_at] // parts).reshape((-1,) + (1,) * (len(dims) - 1 - axis_at))
    return gain


def scatter_about(key, extent, spread, limit, cuts=(), kind=jnp.bfloat16):
    drawn = spread * jax.random.normal(key, extent, jnp.float32)
    if cuts:
        drawn = drawn * block_scale(key, extent, cuts, -0.22, 0.18)
    return jnp.clip(drawn, -limit, limit).astype(kind)


def setup_inputs(seed: int = 0) -> dict:
    seeds = jax.random.split(jax.random.key(seed), 13)
    return {
        "basis_slab": scatter_about(seeds[0], (N, R), 1.0, 6.0, ((0, 32),)),
        "live_counts": draw_live_counts(jax.random.fold_in(seeds[12], 71), 0),
        "pole_order": jax.vmap(lambda own: jax.random.permutation(own, M))(jax.random.split(seeds[2], DEVICES)).reshape((DEVICES, M)).astype(jnp.int32),
        "leaf_diag": scatter_about(seeds[3], (N, M), M ** -0.5, 0.1875, ((0, 32),)),
        "leaf_in": scatter_about(seeds[4], (N, RANK), M ** -0.5, 0.1875, ((0, 32),)),
        "leaf_out": scatter_about(seeds[5], (N, RANK), RANK ** -0.5, 0.5, ((0, 32),)),
        "leaf_lift": scatter_about(seeds[6], (DEVICES, RANK, RANK), (2 * RANK) ** -0.5, 0.375, ((0, 32),)),
        "leaf_couple": scatter_about(seeds[7], (DEVICES, RANK, RANK), RANK ** -0.5, 0.5, ((0, 32),)),
        "leaf_spread": scatter_about(seeds[8], (DEVICES, RANK, RANK), (3 * RANK // 2) ** -0.5, 0.4375, ((0, 32),)),
        "inner_lift": scatter_about(seeds[9], (DEVICES - 4, RANK, RANK), (2 * RANK) ** -0.5, 0.375),
        "inner_couple": scatter_about(seeds[10], (DEVICES - 2, RANK, RANK), RANK ** -0.5, 0.5),
        "inner_spread": scatter_about(seeds[11], (DEVICES - 4, RANK, RANK), (3 * RANK // 2) ** -0.5, 0.4375),
    }


def full_product(matrices, stacked):
    return jnp.einsum('nij,njc->nic', matrices.astype(jnp.float32), stacked, precision=lax.Precision.HIGHEST)


def leaf_skeleton(pieces):
    generator, masked = pieces
    return jnp.einsum('mk,mc->kc', generator, masked, preferred_element_type=jnp.float32)


def leaf_update(pieces):
    diagonal, generator, masked, incoming = pieces
    return jnp.dot(diagonal, masked, preferred_element_type=jnp.float32) + jnp.dot(generator, incoming, preferred_element_type=jnp.float32)


def reference(basis_slab, live_counts, pole_order, leaf_diag, leaf_in, leaf_out, leaf_lift, leaf_couple, leaf_spread, inner_lift, inner_couple, inner_spread):
    devices = N_GRP * N_LEAF
    block_rows = M // devices
    levels = devices.bit_length() - 1
    leaf_rows = basis_slab.reshape(devices, devices, block_rows, R).transpose(1, 0, 2, 3).reshape(devices, M, R)
    slots = jnp.take_along_axis(leaf_rows, pole_order.astype(jnp.int32)[:, :, None], axis=1)
    live_mask = jnp.arange(M, dtype=jnp.int32)[None, :] < live_counts[:, None]
    masked = jnp.where(live_mask[:, :, None], slots, jnp.zeros_like(slots))
    skeleton = lax.map(leaf_skeleton, (leaf_in.reshape(devices, M, RANK), masked))
    crosses = []
    for height in range(levels):
        node_count = devices >> height
        couples = leaf_couple if height == 0 else inner_couple[node_count - 2:2 * node_count - 2]
        coupled = full_product(couples, skeleton)
        crosses.append(coupled.reshape(node_count // 2, 2, RANK, R)[:, ::-1].reshape(node_count, RANK, R))
        if height < levels - 1:
            lifts = leaf_lift if height == 0 else inner_lift[node_count - 4:2 * node_count - 4]
            lifted = full_product(lifts, skeleton)
            skeleton = lifted[0::2] + lifted[1::2]
    incoming = crosses[levels - 1]
    for height in range(levels - 2, -1, -1):
        node_count = devices >> height
        spreads = leaf_spread if height == 0 else inner_spread[node_count - 4:2 * node_count - 4]
        parent = jnp.repeat(incoming, 2, axis=0)
        incoming = full_product(spreads, parent) + crosses[height]
    incoming_b = incoming.astype(jnp.bfloat16)
    updated = lax.map(leaf_update, (leaf_diag.reshape(devices, M, M), leaf_out.reshape(devices, M, RANK), masked, incoming_b))
    updated = jnp.where(live_mask[:, :, None], updated, slots.astype(jnp.float32)).astype(jnp.bfloat16)
    inverse = jnp.zeros((devices, M), jnp.int32).at[jnp.arange(devices, dtype=jnp.int32)[:, None], pole_order.astype(jnp.int32)].set(jnp.broadcast_to(jnp.arange(M, dtype=jnp.int32), (devices, M)))
    restored = jnp.take_along_axis(updated, inverse[:, :, None], axis=1)
    return restored.reshape(devices, devices, block_rows, R).transpose(1, 0, 2, 3).reshape(N, R)
```

```python
import functools

import jax
import jax.numpy as jnp
from jax import lax
from jax.experimental import pallas as pl
from jax.experimental.pallas import tpu as pltpu
from jax.sharding import PartitionSpec as P

MESH = pl.DeviceIdType.MESH
CHUNKS = 4
AHEAD = 2
LEVELS = (5, 6, 7, 8)
PERIOD = 12
FOLD = 1
STARTS = (-9, 3, 16, 27, 39, 53, 65, 96, 2)
ORDER = (8, 4, 7, 3, 2, 5, 6, 1, 0)


def row_dot(a, b):
    return jnp.dot(a, b, preferred_element_type=jnp.float32)


def times(matrix, rows):
    return lax.dot_general(
        rows, matrix, (((1,), (1,)), ((), ())), preferred_element_type=jnp.float32
    )


def fine_times(matrix, rows):
    high = rows.astype(jnp.bfloat16)
    low = (rows - high.astype(jnp.float32)).astype(jnp.bfloat16)
    return times(matrix, high) + times(matrix, low)


def greet(groups, leaves):
    devices = groups * leaves
    me = lax.axis_index("grp") * leaves + lax.axis_index("leaf")
    barrier = pltpu.get_barrier_semaphore()

    def body(shift, carry):
        device = lax.rem(me + shift, devices)
        pl.semaphore_signal(
            barrier,
            inc=1,
            device_id=(lax.div(device, leaves), lax.rem(device, leaves)),
            device_id_type=MESH,
        )
        return carry

    lax.fori_loop(1, devices, body, 0)
    return barrier


def census_kernel(groups, leaves, sizes, live, order, marks, level, table, send, recv):
    devices, tall, lanes = table.shape
    width = order.shape[1]
    block = width // devices
    plane = leaves * block
    per = lanes // block
    group = lax.axis_index("grp")
    seat = lax.axis_index("leaf")
    me = group * leaves + seat
    barrier = greet(groups, leaves)

    slot = lax.broadcasted_iota(jnp.int32, (1, width), 1)
    key = jnp.where(slot < live[...], order[...], -1)
    high = jnp.right_shift(key, lanes.bit_length() - 1)
    low = jnp.bitwise_and(key, lanes - 1)
    high_is = jnp.where(lax.broadcasted_iota(jnp.int32, (tall, width), 0) == high, 1.0, 0.0)
    low_is = jnp.where(lax.broadcasted_iota(jnp.int32, (lanes, width), 0) == low, 1.0, 0.0)
    table[me] = times(low_is.astype(jnp.bfloat16), high_is.astype(jnp.bfloat16))

    pl.semaphore_wait(barrier, devices - 1)

    def body(shift, carry):
        device = lax.rem(me + shift, devices)
        pltpu.make_async_remote_copy(
            src_ref=table.at[me],
            dst_ref=table.at[me],
            send_sem=send,
            recv_sem=recv,
            device_id=(lax.div(device, leaves), lax.rem(device, leaves)),
            device_id_type=MESH,
        ).start()
        return carry

    lax.fori_loop(1, devices, body, 0)
    lane = lax.broadcasted_iota(jnp.int32, (lanes, lanes), 0)
    bucket = jnp.where(
        lax.div(lane, block) == lax.broadcasted_iota(jnp.int32, (lanes, lanes), 1), 1.0, 0.0
    ).astype(jnp.bfloat16)
    lane = lax.broadcasted_iota(jnp.int32, (lanes, plane), 0)
    row = lax.broadcasted_iota(jnp.int32, (lanes, plane), 1)
    spread = jnp.where(
        lane == lax.rem(seat, per) * block + lax.rem(row, block), 1.0, 0.0
    ).astype(jnp.bfloat16)
    before = jnp.where(
        lax.broadcasted_iota(jnp.int32, (plane, plane), 0)
        < lax.broadcasted_iota(jnp.int32, (plane, plane), 1),
        1.0,
        0.0,
    ).astype(jnp.bfloat16)
    few = table.at[pl.ds(0, devices - 1)]
    pltpu.make_async_copy(few, few, recv).wait()

    owner = lax.broadcasted_iota(jnp.int32, (tall, lanes), 0) * per + lax.broadcasted_iota(
        jnp.int32, (tall, lanes), 1
    )
    inside = lax.broadcasted_iota(jnp.int32, (tall, lanes), 1) < per
    most = jnp.zeros((tall, lanes), jnp.float32)
    for target in range(groups):
        total = jnp.sum(table[target * leaves : (target + 1) * leaves], axis=0)
        counts = row_dot(total.astype(jnp.bfloat16), bucket)
        away = inside & (lax.div(owner, leaves) != target)
        most = jnp.maximum(most, jnp.where(away, counts, 0.0))
    largest = jnp.max(most)
    pick = jnp.int32(0)
    for size in sizes[:-1]:
        pick = pick + jnp.where(largest > size, 1, 0).astype(jnp.int32)
    level[0, 0] = pick

    def strip(first_leaf, device):
        rows = table[pl.ds(first_leaf, leaves)]
        at = lax.broadcasted_iota(jnp.int32, rows.shape, 1)
        return jnp.sum(jnp.where(at == lax.div(device, per), rows, 0.0), axis=1)

    strips = []
    for apart in range(groups):
        strips.append(strip(lax.rem(group - apart + groups, groups) * leaves, me))
    for apart in range(groups):
        other = lax.rem(group + apart, groups)
        strips.append(strip(group * leaves, other * leaves + seat))
    wide = row_dot(jnp.concatenate(strips, axis=0).astype(jnp.bfloat16), spread)
    leaf = lax.rem(lax.broadcasted_iota(jnp.int32, wide.shape, 0), leaves)
    here = leaf == lax.div(lax.broadcasted_iota(jnp.int32, wide.shape, 1), block)
    flags = jnp.sum(jnp.where(here, wide, 0.0).reshape(2 * groups, leaves, plane), axis=1)
    ranks = row_dot(flags.astype(jnp.bfloat16), before)
    marks[...] = jnp.where(flags > 0.5, ranks, -1.0)
    pltpu.make_async_copy(few, few, send).wait()


def fused_kernel(
    groups,
    leaves,
    slab,
    live,
    order,
    marks,
    diag,
    gen_in,
    gen_out,
    leaf_lift,
    leaf_couple,
    leaf_spread,
    inner_lift,
    inner_couple,
    inner_spread,
    out,
    slab_here,
    pack_at,
    unpack_at,
    gone,
    there_sent,
    there_got,
    relay_in,
    arrived,
    staged,
    relay_out,
    back_sent,
    back_got,
    out_here_rows,
    diag_here,
    in_here,
    out_here,
    lifts,
    couples,
    spreads,
    lift_here,
    couple_here,
    spread_here,
    pair_sent,
    pair_got,
    select,
    diag_poles,
    in_poles,
    out_poles,
    up_sent,
    up_got,
    top,
    cross,
    down_sent,
    down_got,
    slab_sem,
    z_send,
    z_recv,
    in_send,
    in_recv,
    out_send,
    out_recv,
    tree_send,
    tree_recv,
    local_sem,
    store_sem,
    load_sem,
    pair_send,
    pair_recv,
):
    devices = groups * leaves
    chunks, width, cols = arrived.shape
    size = there_sent.shape[2]
    block = width // devices
    plane = leaves * block
    share = groups * block
    part_cols = cols // leaves
    group = lax.axis_index("grp")
    seat = lax.axis_index("leaf")

    def seats(step):
        def body(shift, carry):
            step(lax.rem(seat + shift, leaves))
            return carry

        lax.fori_loop(1, leaves, body, 0)

    def cols_of(chunk):
        return pl.ds(pl.multiple_of(chunk * cols, cols), cols)

    def below(apart):
        return lax.rem(group - apart + groups, groups)

    def above(apart):
        return lax.rem(group + apart, groups)

    def plane_rows(which):
        return pl.ds(pl.multiple_of(which * plane, plane), plane)

    def leaf_rows(which, other):
        return pl.ds(pl.multiple_of(which * plane + other * block, block), block)

    def part_rows(index):
        return pl.ds(pl.multiple_of(index * block, block), block)

    def share_part(other, apart):
        return pl.ds(pl.multiple_of(other * share + apart * block, block), block)

    barrier = greet(groups, leaves)

    def slab_load(chunk):
        return pltpu.make_async_copy(
            slab.at[:, cols_of(chunk)], slab_here.at[chunk], slab_sem.at[chunk]
        )

    def each(low, high, step):
        def body(index, carry):
            step(index)
            return carry

        lax.fori_loop(low, high, body, 0)

    each(0, chunks, lambda chunk: slab_load(chunk).start())

    pairs = [(diag, diag_here), (gen_in, in_here), (gen_out, out_here)]
    pairs += [(inner_lift, lifts), (inner_couple, couples), (inner_spread, spreads)]
    pairs += [(leaf_lift.at[0], lift_here), (leaf_couple.at[0], couple_here)]
    pairs += [(leaf_spread.at[0], spread_here)]
    loads = [
        pltpu.make_async_copy(source, target, load_sem.at[index])
        for index, (source, target) in enumerate(pairs)
    ]
    for load in loads:
        load.start()

    turned = marks[...].T
    row = lax.broadcasted_iota(jnp.int32, (size, plane), 0).astype(jnp.float32)
    lane = lax.broadcasted_iota(jnp.int32, (plane, size), 1).astype(jnp.float32)

    def along(role):
        return jnp.where(row == marks[role : role + 1, :], 1.0, 0.0).astype(jnp.bfloat16)

    def across(role):
        return jnp.where(lane == turned[:, role : role + 1], 1.0, 0.0).astype(jnp.bfloat16)

    for apart in range(1, groups):
        pack_at[0, apart - 1] = along(apart)
    pl.semaphore_wait(barrier, devices - 1)

    def z_copy(source, target, way, chunk, apart, device):
        return pltpu.make_async_remote_copy(
            src_ref=source,
            dst_ref=target,
            send_sem=z_send.at[way, chunk, apart - 1],
            recv_sem=z_recv.at[way, chunk, apart - 1],
            device_id=(device, seat),
            device_id_type=MESH,
        )

    def send_there(chunk, apart):
        return z_copy(
            there_sent.at[chunk, apart - 1],
            there_got.at[chunk, apart - 1],
            0,
            chunk,
            apart,
            below(apart),
        )

    def send_back(chunk, apart):
        return z_copy(
            back_sent.at[chunk, apart - 1],
            back_got.at[chunk, apart - 1],
            1,
            chunk,
            apart,
            above(apart),
        )

    def deliver(source, chunk, apart):
        target = arrived.at[chunk, share_part(seat, apart)]
        seats(
            lambda other: pltpu.make_async_remote_copy(
                src_ref=source(other),
                dst_ref=target,
                send_sem=in_send.at[apart, chunk],
                recv_sem=in_recv.at[apart, chunk],
                device_id=(group, other),
                device_id_type=MESH,
            ).start()
        )
        pltpu.make_async_copy(source(seat), target, local_sem.at[0, apart, chunk]).start()

    def send_in(chunk):
        slab_load(chunk).wait()

        def pack(apart):
            there_sent[chunk, apart - 1] = row_dot(
                pack_at[0, apart - 1], slab_here[chunk, plane_rows(below(apart)), :]
            ).astype(jnp.bfloat16)
            send_there(chunk, apart).start()

        each(1, groups, pack)
        deliver(lambda other: slab.at[leaf_rows(group, other), cols_of(chunk)], chunk, 0)

    def wait_bytes(buffer, chunk, rows, semaphore):
        part = buffer.at[chunk, pl.ds(0, rows)]
        pltpu.make_async_copy(part, part, semaphore).wait()

    def relay_there(index):
        chunk = lax.div(index, groups - 1)
        apart = lax.rem(index, groups - 1) + 1
        send_there(chunk, apart).wait_recv()
        relay_in[chunk, apart - 1] = row_dot(
            unpack_at[0, apart - 1], there_got[chunk, apart - 1]
        ).astype(jnp.bfloat16)
        deliver(lambda other: relay_in.at[chunk, apart - 1, part_rows(other)], chunk, apart)

    def send_out(chunk):
        def go(index):
            apart = lax.rem(index + 1, groups)
            target = relay_out.at[chunk, apart, part_rows(seat)]
            seats(
                lambda other: pltpu.make_async_remote_copy(
                    src_ref=staged.at[chunk, share_part(other, apart)],
                    dst_ref=target,
                    send_sem=out_send.at[apart, chunk],
                    recv_sem=out_recv.at[apart, chunk],
                    device_id=(group, other),
                    device_id_type=MESH,
                ).start()
            )
            pltpu.make_async_copy(
                staged.at[chunk, share_part(seat, apart)], target, local_sem.at[1, apart, chunk]
            ).start()

        each(0, groups, go)

    def wait_back(chunk, apart):
        wait_bytes(staged, chunk, (leaves - 1) * block, out_recv.at[apart, chunk])
        wait_bytes(staged, chunk, block, local_sem.at[1, apart, chunk])

    def relay_back(index):
        chunk = lax.div(index, groups - 1)
        apart = lax.rem(index, groups - 1) + 1
        wait_back(chunk, apart)
        back_sent[chunk, apart - 1] = row_dot(
            pack_at[1, apart - 1], relay_out[chunk, apart]
        ).astype(jnp.bfloat16)
        send_back(chunk, apart).start()

    def put(chunk, apart, rows):
        which = plane_rows(below(apart))
        kept = slab_here[chunk, which, :].astype(jnp.float32)
        out_here_rows[chunk, which, :] = (rows + gone[apart] * kept).astype(jnp.bfloat16)

    def stores(chunk):
        return pltpu.make_async_copy(
            out_here_rows.at[chunk], out.at[:, cols_of(chunk)], store_sem.at[chunk]
        )

    def settle(index):
        chunk = lax.div(index, groups - 1)
        apart = lax.rem(index, groups - 1) + 1

        @pl.when(apart == 1)
        def near():
            wait_back(chunk, 0)
            put(chunk, 0, relay_out[chunk, 0].astype(jnp.float32))

        send_back(chunk, apart).wait_recv()
        put(chunk, apart, row_dot(unpack_at[1, apart - 1], back_got[chunk, apart - 1]))

        @pl.when(apart == groups - 1)
        def done():
            stores(chunk).start()

    def tree_copy(source, target, chunk, stage, device):
        return pltpu.make_async_remote_copy(
            src_ref=source,
            dst_ref=target,
            send_sem=tree_send.at[stage, chunk],
            recv_sem=tree_recv.at[stage, chunk],
            device_id=device,
            device_id_type=MESH,
        )

    each(0, min(AHEAD, chunks), send_in)

    for apart in range(1, groups):
        unpack_at[0, apart - 1] = across(groups + apart)
        pack_at[1, apart - 1] = along(groups + apart)
        unpack_at[1, apart - 1] = across(apart)
    for apart in range(groups):
        gone[apart] = jnp.where(turned[:, apart : apart + 1] < 0.0, 1.0, 0.0)

    slot = lax.broadcasted_iota(jnp.int32, (1, width), 1)
    pole = order[...]
    apart = lax.rem(lax.div(pole, plane) - group + groups, groups)
    inner = lax.rem(pole, plane)
    moved = lax.div(inner, block) * share + apart * block + lax.rem(inner, block)
    key = jnp.where(slot < live[...], moved, -1)
    part = min(256, width)
    for start in range(0, width, part):
        pole = lax.broadcasted_iota(jnp.int32, (part, width), 0) + start
        select[start : start + part, :] = jnp.where(pole == key, 1.0, 0.0).astype(jnp.bfloat16)

    for load in loads:
        load.wait()

    def fold(index, carry):
        start = pl.multiple_of(index * part, part)
        rows = pl.ds(start, part)
        chosen = select[rows, :]
        out_poles[rows, :] = row_dot(chosen, out_here[...]).astype(jnp.bfloat16)
        in_poles[rows, :] = row_dot(chosen, in_here[...])
        return carry

    lax.fori_loop(0, width // part, fold, 0)
    gather = in_poles[...].T.astype(jnp.bfloat16)

    def fold_diag(index):
        rows = pl.ds(pl.multiple_of(index * part, part), part)
        half = row_dot(select[rows, :], diag_here[...]).astype(jnp.bfloat16)
        full = lax.dot_general(
            half, select[...], (((1,), (1,)), ((), ())), preferred_element_type=jnp.float32
        )
        diag_poles[rows, :] = full.astype(jnp.bfloat16)

    def seat_rows(other):
        return pl.ds(pl.multiple_of(other * part_cols, part_cols), part_cols)

    def wait_up(chunk, semaphore):
        most = up_got.at[chunk, pl.ds(0, leaves - 1)]
        pltpu.make_async_copy(most, most, semaphore).wait()

    def wait_top(chunk, semaphore):
        most = top.at[chunk, pl.ds(0, groups - 1)]
        pltpu.make_async_copy(most, most, semaphore).wait()

    def wait_down(chunk, semaphore):
        most = down_got.at[chunk, pl.ds(0, cols - part_cols)]
        pltpu.make_async_copy(most, most, semaphore).wait()

    def node(local):
        depth = local.bit_length() - 1
        return (groups + group) * (1 << depth) + (local - (1 << depth))

    def lift_of(local):
        return lifts[node(local) - 4]

    def couple_of(local):
        return couples[node(local) - 2]

    def spread_of(local):
        return spreads[node(local) - 4]

    def pair_copy(chunk):
        return pltpu.make_async_remote_copy(
            src_ref=pair_sent.at[chunk],
            dst_ref=pair_got.at[chunk],
            send_sem=pair_send.at[chunk],
            recv_sem=pair_recv.at[chunk],
            device_id=(group, seat + 1 - 2 * lax.rem(seat, 2)),
            device_id_type=MESH,
        )

    def first(chunk):
        def ready(apart):
            wait_bytes(arrived, chunk, (leaves - 1) * block, in_recv.at[apart, chunk])
            wait_bytes(arrived, chunk, block, local_sem.at[0, apart, chunk])

        each(0, groups, ready)
        skeleton = row_dot(gather, arrived[chunk]).T
        up_sent[chunk] = fine_times(lift_here[...], skeleton).astype(jnp.bfloat16)
        seats(
            lambda other: tree_copy(
                up_sent.at[chunk, seat_rows(other)], up_got.at[chunk, seat], chunk, 0, (group, other)
            ).start()
        )
        up_got[chunk, seat] = up_sent[chunk, seat_rows(seat), :]
        pair_sent[chunk] = fine_times(couple_here[...], skeleton).astype(jnp.bfloat16)
        pair_copy(chunk).start()

    def second(chunk):
        wait_up(chunk, tree_recv.at[0, chunk])
        skeletons = {}
        for index in range(leaves // 2):
            left = up_got[chunk, 2 * index].astype(jnp.float32)
            right = up_got[chunk, 2 * index + 1].astype(jnp.float32)
            skeletons[leaves // 2 + index] = (left + right).astype(jnp.bfloat16)
        for local in range(leaves - 1, 1, -1):
            cross[chunk, local ^ 1] = times(couple_of(local), skeletons[local])
            if local % 2 == 0:
                skeletons[local // 2] = (
                    times(lift_of(local), skeletons[local])
                    + times(lift_of(local + 1), skeletons[local + 1])
                ).astype(jnp.bfloat16)
        top[chunk, groups + group] = skeletons[1]

        def body(shift, carry):
            tree_copy(
                top.at[chunk, groups + group],
                top.at[chunk, groups + group],
                chunk,
                1,
                (lax.rem(group + shift, groups), seat),
            ).start()
            return carry

        lax.fori_loop(1, groups, body, 0)

    def third(chunk):
        wait_top(chunk, tree_recv.at[1, chunk])
        for index in range(groups - 1, 1, -1):
            top[chunk, index] = (
                times(lifts[2 * index - 4], top[chunk, 2 * index])
                + times(lifts[2 * index - 3], top[chunk, 2 * index + 1])
            ).astype(jnp.bfloat16)
        incoming = None
        for height in range(groups.bit_length() - 2, -1, -1):
            mine = lax.div(groups + group, 1 << height)
            other = mine + 1 - 2 * lax.rem(mine, 2)
            crossed = times(couples[other - 2], top[chunk, other])
            if incoming is not None:
                crossed = crossed + fine_times(spreads[mine - 4], incoming)
            incoming = crossed
        passed = {1: incoming}
        for local in range(2, leaves):
            passed[local] = (
                fine_times(spread_of(local), passed[local // 2]) + cross[chunk, local]
            )
        for index in range(leaves // 2):
            down_sent[chunk, index] = passed[leaves // 2 + index].astype(jnp.bfloat16)
        seats(
            lambda other: tree_copy(
                down_sent.at[chunk, lax.div(other, 2)],
                down_got.at[chunk, seat_rows(seat)],
                chunk,
                2,
                (group, other),
            ).start()
        )
        down_got[chunk, seat_rows(seat), :] = down_sent[chunk, lax.div(seat, 2)]

    def finish(chunk):
        wait_down(chunk, tree_recv.at[2, chunk])
        pair_copy(chunk).wait_recv()
        incoming = times(spread_here[...], down_got[chunk]) + pair_got[chunk].astype(jnp.float32)
        incoming = incoming.T.astype(jnp.bfloat16)

        def rows_done(index, carry):
            rows = pl.ds(pl.multiple_of(index * part, part), part)
            value = row_dot(diag_poles[rows, :], arrived[chunk]) + row_dot(
                out_poles[rows, :], incoming
            )
            staged[chunk, rows, :] = value.astype(jnp.bfloat16)
            return carry

        lax.fori_loop(0, width // part, rows_done, 0)
        send_out(chunk)

    stages = (send_in, relay_there, first, second, third, finish, relay_back, settle, fold_diag)

    parts = (1, groups - 1, 1, 1, 1, 1, groups - 1, groups - 1, 1)
    counts = [chunks * pieces for pieces in parts[:-1]] + [width // part]

    def tick(now):
        for stage in ORDER:
            since = now - STARTS[stage]
            step = FOLD if stage == 8 else PERIOD // parts[stage]
            index = lax.div(since, step)
            lowest = AHEAD if stage == 0 else 0
            due = (lax.rem(since, step) == 0) & (since >= 0)

            @pl.when(due & (index >= lowest) & (index < counts[stage]))
            def run():
                stages[stage](index)

    last = max(
        start + (count - 1) * (PERIOD // pieces)
        for start, count, pieces in zip(STARTS, counts[:-1], parts)
    )
    each(0, last + 1, tick)


    def drain(chunk):
        for apart in range(1, groups):
            send_there(chunk, apart).wait_send()
            send_back(chunk, apart).wait_send()
        for apart in range(groups):
            wait_bytes(arrived, chunk, (leaves - 1) * block, in_send.at[apart, chunk])
            wait_bytes(staged, chunk, (leaves - 1) * block, out_send.at[apart, chunk])
        wait_up(chunk, tree_send.at[0, chunk])
        wait_top(chunk, tree_send.at[1, chunk])
        wait_down(chunk, tree_send.at[2, chunk])
        pair_copy(chunk).wait_send()
        stores(chunk).wait()

    each(0, chunks, drain)


def fused(
    basis_slab,
    live_counts,
    pole_order,
    leaf_diag,
    leaf_in,
    leaf_out,
    leaf_lift,
    leaf_couple,
    leaf_spread,
    inner_lift,
    inner_couple,
    inner_spread,
):
    groups = lax.axis_size("grp")
    leaves = lax.axis_size("leaf")
    devices = groups * leaves
    width, slab_rows = basis_slab.shape
    block = width // devices
    plane = leaves * block
    rank = leaf_in.shape[1]
    cols = slab_rows // CHUNKS
    vmem = pl.BlockSpec(memory_space=pltpu.VMEM)
    smem = pl.BlockSpec(memory_space=pltpu.SMEM)
    anywhere = pl.BlockSpec(memory_space=pl.ANY)
    half = jnp.bfloat16
    sizes = tuple(plane * level // LEVELS[-1] for level in LEVELS)
    counts = live_counts.reshape(1, 1)
    lanes = 128
    marks, level = pl.pallas_call(
        functools.partial(census_kernel, groups, leaves, sizes),
        out_shape=[
            jax.ShapeDtypeStruct((2 * groups, plane), jnp.float32),
            jax.ShapeDtypeStruct((1, 1), jnp.int32),
        ],
        in_specs=[vmem] * 2,
        out_specs=[vmem, smem],
        scratch_shapes=[
            pltpu.VMEM((devices, width // lanes, lanes), jnp.float32),
            pltpu.SemaphoreType.DMA,
            pltpu.SemaphoreType.DMA,
        ],
        compiler_params=pltpu.CompilerParams(collective_id=0, has_side_effects=True),
    )(counts, pole_order)

    def main(index):
        size = sizes[index]
        away = groups - 1
        return pl.pallas_call(
            functools.partial(fused_kernel, groups, leaves),
            out_shape=jax.ShapeDtypeStruct((width, slab_rows), half),
            in_specs=[anywhere] + [vmem] * 3 + [anywhere] * 9,
            out_specs=anywhere,
            scratch_shapes=[
                pltpu.VMEM((CHUNKS, width, cols), half),
                pltpu.VMEM((2, away, size, plane), half),
                pltpu.VMEM((2, away, plane, size), half),
                pltpu.VMEM((groups, plane, 1), jnp.float32),
                pltpu.VMEM((CHUNKS, away, size, cols), half),
                pltpu.VMEM((CHUNKS, away, size, cols), half),
                pltpu.VMEM((CHUNKS, away, plane, cols), half),
                pltpu.VMEM((CHUNKS, width, cols), half),
                pltpu.VMEM((CHUNKS, width, cols), half),
                pltpu.VMEM((CHUNKS, groups, plane, cols), half),
                pltpu.VMEM((CHUNKS, away, size, cols), half),
                pltpu.VMEM((CHUNKS, away, size, cols), half),
                pltpu.VMEM((CHUNKS, width, cols), half),
                pltpu.VMEM((width, width), half),
                pltpu.VMEM((width, rank), half),
                pltpu.VMEM((width, rank), half),
                pltpu.VMEM(inner_lift.shape, half),
                pltpu.VMEM(inner_couple.shape, half),
                pltpu.VMEM(inner_spread.shape, half),
                pltpu.VMEM((rank, rank), half),
                pltpu.VMEM((rank, rank), half),
                pltpu.VMEM((rank, rank), half),
                pltpu.VMEM((CHUNKS, cols, rank), half),
                pltpu.VMEM((CHUNKS, cols, rank), half),
                pltpu.VMEM((width, width), half),
                pltpu.VMEM((width, width), half),
                pltpu.VMEM((width, rank), jnp.float32),
                pltpu.VMEM((width, rank), half),
                pltpu.VMEM((CHUNKS, cols, rank), half),
                pltpu.VMEM((CHUNKS, leaves, cols // leaves, rank), half),
                pltpu.VMEM((CHUNKS, 2 * groups, cols // leaves, rank), half),
                pltpu.VMEM((CHUNKS, leaves, cols // leaves, rank), jnp.float32),
                pltpu.VMEM((CHUNKS, leaves // 2, cols // leaves, rank), half),
                pltpu.VMEM((CHUNKS, cols, rank), half),
                pltpu.SemaphoreType.DMA((CHUNKS,)),
                pltpu.SemaphoreType.DMA((2, CHUNKS, away)),
                pltpu.SemaphoreType.DMA((2, CHUNKS, away)),
                pltpu.SemaphoreType.DMA((groups, CHUNKS)),
                pltpu.SemaphoreType.DMA((groups, CHUNKS)),
                pltpu.SemaphoreType.DMA((groups, CHUNKS)),
                pltpu.SemaphoreType.DMA((groups, CHUNKS)),
                pltpu.SemaphoreType.DMA((3, CHUNKS)),
                pltpu.SemaphoreType.DMA((3, CHUNKS)),
                pltpu.SemaphoreType.DMA((2, groups, CHUNKS)),
                pltpu.SemaphoreType.DMA((CHUNKS,)),
                pltpu.SemaphoreType.DMA((9,)),
                pltpu.SemaphoreType.DMA((CHUNKS,)),
                pltpu.SemaphoreType.DMA((CHUNKS,)),
            ],
            compiler_params=pltpu.CompilerParams(
                collective_id=1 + index, has_side_effects=True, vmem_limit_bytes=56 * 1024 * 1024
            ),
        )(
            basis_slab,
            counts,
            pole_order,
            marks,
            leaf_diag,
            leaf_in,
            leaf_out,
            leaf_lift,
            leaf_couple,
            leaf_spread,
            inner_lift,
            inner_couple,
            inner_spread,
        )

    branches = [functools.partial(main, index) for index in range(len(sizes))]
    return lax.switch(level[0, 0], branches)


def from_partner(block, axis, apart):
    count = lax.axis_size(axis)
    route = []
    for low in range(count):
        high = low | 1 << apart
        if high != low and high < count:
            route += [(low, high), (high, low)]
    return lax.ppermute(block, axis, route)


def transform(matrix, stacked):
    return jnp.dot(matrix.astype(jnp.float32), stacked, precision=lax.Precision.HIGHEST)


def local(
    basis_slab,
    live_counts,
    pole_order,
    leaf_diag,
    leaf_in,
    leaf_out,
    leaf_lift,
    leaf_couple,
    leaf_spread,
    inner_lift,
    inner_couple,
    inner_spread,
):
    groups = lax.axis_size("grp")
    leaves = lax.axis_size("leaf")
    devices = groups * leaves
    leaf_width = basis_slab.shape[0]
    slab_rows = basis_slab.shape[1]
    block_rows = leaf_width // devices
    levels = devices.bit_length() - 1
    leaf_bits = leaves.bit_length() - 1
    position = lax.axis_index("grp") * leaves + lax.axis_index("leaf")

    def redistribute(columns):
        arrived = lax.all_to_all(
            columns.reshape(devices, block_rows, slab_rows),
            ("grp", "leaf"),
            split_axis=0,
            concat_axis=0,
            tiled=True,
        )
        return arrived.reshape(leaf_width, slab_rows)

    def node_matrix(height, leaf_table, inner_table, offset):
        if height == 0:
            return leaf_table[0]
        own_node = jnp.right_shift(devices + position, height)
        return lax.dynamic_index_in_dim(inner_table, own_node - offset, 0, keepdims=False)

    leaf_rows = redistribute(basis_slab)
    slot_order = pole_order[0]
    live_count = live_counts[0]
    slots = jnp.take(leaf_rows, slot_order, axis=0)
    live_mask = jnp.arange(leaf_width, dtype=jnp.int32) < live_count
    masked = jnp.where(live_mask[:, None], slots, jnp.zeros_like(slots))
    skeleton = jnp.einsum("mk,mc->kc", leaf_in, masked, preferred_element_type=jnp.float32)
    crosses = []
    for height in range(leaf_bits):
        lifted = transform(node_matrix(height, leaf_lift, inner_lift, 4), skeleton)
        coupled = transform(node_matrix(height, leaf_couple, inner_couple, 2), skeleton)
        other_lift, other_cross = from_partner((lifted, coupled), "leaf", height)
        crosses.append(other_cross)
        skeleton = lifted + other_lift
    group_bits = groups.bit_length() - 1
    for height in range(leaf_bits, levels - 1):
        lifted = transform(node_matrix(height, leaf_lift, inner_lift, 4), skeleton)
        coupled = transform(node_matrix(height, leaf_couple, inner_couple, 2), skeleton)
        other_lift, other_cross = (
            from_partner(lifted.astype(jnp.bfloat16), "grp", height - leaf_bits).astype(
                lifted.dtype
            ),
            from_partner(coupled.astype(jnp.bfloat16), "grp", height - leaf_bits).astype(
                coupled.dtype
            ),
        )
        crosses.append(other_cross)
        skeleton = lifted + other_lift
    coupled = transform(node_matrix(levels - 1, leaf_couple, inner_couple, 2), skeleton)
    crosses.append(
        from_partner(coupled.astype(jnp.bfloat16), "grp", group_bits - 1).astype(coupled.dtype)
    )
    incoming = crosses[levels - 1]
    for height in range(levels - 2, -1, -1):
        incoming = (
            transform(node_matrix(height, leaf_spread, inner_spread, 4), incoming) + crosses[height]
        )
    incoming_b = incoming.astype(jnp.bfloat16)
    tile_rows = leaf_width // 8
    tile_count = live_count // tile_rows

    def one_tile(tile_index, merged_rows):
        row_start = tile_index * tile_rows
        diag_rows = lax.dynamic_slice_in_dim(leaf_diag, row_start, tile_rows, 0)
        out_rows = lax.dynamic_slice_in_dim(leaf_out, row_start, tile_rows, 0)
        value = jnp.dot(diag_rows, masked, preferred_element_type=jnp.float32) + jnp.dot(
            out_rows, incoming_b, preferred_element_type=jnp.float32
        )
        return lax.dynamic_update_slice_in_dim(merged_rows, value, row_start, 0)

    merged_rows = lax.fori_loop(
        0, tile_count, one_tile, jnp.zeros((leaf_width, slab_rows), jnp.float32)
    )
    updated = jnp.where(live_mask[:, None], merged_rows, slots.astype(jnp.float32)).astype(
        jnp.bfloat16
    )
    inverse = (
        jnp.zeros((leaf_width,), jnp.int32)
        .at[slot_order]
        .set(jnp.arange(leaf_width, dtype=jnp.int32))
    )
    restored = jnp.take(updated, inverse, axis=0)
    return redistribute(restored)


def solution(mesh):
    placed = (
        P(("grp", "leaf"), None),
        P(("grp", "leaf")),
        P(("grp", "leaf"), None),
        P(("grp", "leaf"), None),
        P(("grp", "leaf"), None),
        P(("grp", "leaf"), None),
        P(("grp", "leaf"), None, None),
        P(("grp", "leaf"), None, None),
        P(("grp", "leaf"), None, None),
        P(),
        P(),
        P(),
    )

    def step(basis_slab, *rest):
        devices = mesh.shape["grp"] * mesh.shape["leaf"]
        block_rows = basis_slab.shape[0] // devices
        whole_tiles = (
            block_rows % 16 == 0
            and 128 % block_rows == 0
            and mesh.shape["leaf"] % (128 // block_rows) == 0
            and basis_slab.shape[1] % (128 * CHUNKS) == 0
            and basis_slab.shape[1] % (16 * CHUNKS * mesh.shape["leaf"]) == 0
        )
        return (fused if whole_tiles else local)(basis_slab, *rest)

    return jax.shard_map(
        step, mesh=mesh, in_specs=placed, out_specs=P(("grp", "leaf"), None), check_vma=False
    )
```

```python
import functools

import jax
import jax.numpy as jnp
from jax import lax
from jax.experimental import pallas as pl
from jax.experimental.pallas import tpu as pltpu
from jax.sharding import PartitionSpec as P

MESH = pl.DeviceIdType.MESH
CHUNKS = 8
AHEAD = 4
LEVELS = (8, 9, 10, 11, 12, 13, 14, 16)
PERIOD = 12
STARTS = (-9, 11, 35, 51, 70, 85, 98, 121, 14)
ORDER = (4, 8, 7, 2, 5, 3, 0, 1, 6)


def row_dot(a, b):
    return jnp.dot(a, b, preferred_element_type=jnp.float32)


def times(matrix, rows):
    return lax.dot_general(
        rows, matrix, (((1,), (1,)), ((), ())), preferred_element_type=jnp.float32
    )


def fine_times(matrix, rows):
    high = rows.astype(jnp.bfloat16)
    low = (rows - high.astype(jnp.float32)).astype(jnp.bfloat16)
    return times(matrix, high) + times(matrix, low)


def greet(groups, leaves):
    devices = groups * leaves
    me = lax.axis_index("grp") * leaves + lax.axis_index("leaf")
    barrier = pltpu.get_barrier_semaphore()

    def body(shift, carry):
        device = lax.rem(me + shift, devices)
        pl.semaphore_signal(
            barrier,
            inc=1,
            device_id=(lax.div(device, leaves), lax.rem(device, leaves)),
            device_id_type=MESH,
        )
        return carry

    lax.fori_loop(1, devices, body, 0)
    return barrier


def census_kernel(groups, leaves, sizes, live, order, marks, level, table, send, recv):
    devices, tall, lanes = table.shape
    width = order.shape[1]
    block = width // devices
    plane = leaves * block
    per = lanes // block
    group = lax.axis_index("grp")
    seat = lax.axis_index("leaf")
    me = group * leaves + seat
    barrier = greet(groups, leaves)

    slot = lax.broadcasted_iota(jnp.int32, (1, width), 1)
    key = jnp.where(slot < live[...], order[...], -1)
    high = jnp.right_shift(key, lanes.bit_length() - 1)
    low = jnp.bitwise_and(key, lanes - 1)
    high_is = jnp.where(lax.broadcasted_iota(jnp.int32, (tall, width), 0) == high, 1.0, 0.0)
    low_is = jnp.where(lax.broadcasted_iota(jnp.int32, (lanes, width), 0) == low, 1.0, 0.0)
    table[me] = times(low_is.astype(jnp.bfloat16), high_is.astype(jnp.bfloat16))

    pl.semaphore_wait(barrier, devices - 1)

    def body(shift, carry):
        device = lax.rem(me + shift, devices)
        pltpu.make_async_remote_copy(
            src_ref=table.at[me],
            dst_ref=table.at[me],
            send_sem=send,
            recv_sem=recv,
            device_id=(lax.div(device, leaves), lax.rem(device, leaves)),
            device_id_type=MESH,
        ).start()
        return carry

    lax.fori_loop(1, devices, body, 0)
    lane = lax.broadcasted_iota(jnp.int32, (lanes, lanes), 0)
    bucket = jnp.where(
        lax.div(lane, block) == lax.broadcasted_iota(jnp.int32, (lanes, lanes), 1), 1.0, 0.0
    ).astype(jnp.bfloat16)
    lane = lax.broadcasted_iota(jnp.int32, (lanes, plane), 0)
    row = lax.broadcasted_iota(jnp.int32, (lanes, plane), 1)
    spread = jnp.where(
        lane == lax.rem(seat, per) * block + lax.rem(row, block), 1.0, 0.0
    ).astype(jnp.bfloat16)
    before = jnp.where(
        lax.broadcasted_iota(jnp.int32, (plane, plane), 0)
        < lax.broadcasted_iota(jnp.int32, (plane, plane), 1),
        1.0,
        0.0,
    ).astype(jnp.bfloat16)
    few = table.at[pl.ds(0, devices - 1)]
    pltpu.make_async_copy(few, few, recv).wait()

    owner = lax.broadcasted_iota(jnp.int32, (tall, lanes), 0) * per + lax.broadcasted_iota(
        jnp.int32, (tall, lanes), 1
    )
    inside = lax.broadcasted_iota(jnp.int32, (tall, lanes), 1) < per
    most = jnp.zeros((tall, lanes), jnp.float32)
    for target in range(groups):
        total = jnp.sum(table[target * leaves : (target + 1) * leaves], axis=0)
        counts = row_dot(total.astype(jnp.bfloat16), bucket)
        away = inside & (lax.div(owner, leaves) != target)
        most = jnp.maximum(most, jnp.where(away, counts, 0.0))
    largest = jnp.max(most)
    pick = jnp.int32(0)
    for size in sizes[:-1]:
        pick = pick + jnp.where(largest > size, 1, 0).astype(jnp.int32)
    level[0, 0] = pick

    def strip(first_leaf, device):
        rows = table[pl.ds(first_leaf, leaves)]
        at = lax.broadcasted_iota(jnp.int32, rows.shape, 1)
        return jnp.sum(jnp.where(at == lax.div(device, per), rows, 0.0), axis=1)

    strips = []
    for apart in range(groups):
        strips.append(strip(lax.rem(group - apart + groups, groups) * leaves, me))
    for apart in range(groups):
        other = lax.rem(group + apart, groups)
        strips.append(strip(group * leaves, other * leaves + seat))
    wide = row_dot(jnp.concatenate(strips, axis=0).astype(jnp.bfloat16), spread)
    leaf = lax.rem(lax.broadcasted_iota(jnp.int32, wide.shape, 0), leaves)
    here = leaf == lax.div(lax.broadcasted_iota(jnp.int32, wide.shape, 1), block)
    flags = jnp.sum(jnp.where(here, wide, 0.0).reshape(2 * groups, leaves, plane), axis=1)
    ranks = row_dot(flags.astype(jnp.bfloat16), before)
    marks[...] = jnp.where(flags > 0.5, ranks, -1.0)
    pltpu.make_async_copy(few, few, send).wait()


def fused_kernel(
    groups,
    leaves,
    slab,
    live,
    order,
    marks,
    diag,
    gen_in,
    gen_out,
    leaf_lift,
    leaf_couple,
    leaf_spread,
    inner_lift,
    inner_couple,
    inner_spread,
    out,
    slab_here,
    pack_at,
    unpack_at,
    gone,
    there_sent,
    there_got,
    relay_in,
    arrived,
    staged,
    relay_out,
    back_sent,
    back_got,
    out_here_rows,
    diag_here,
    in_here,
    out_here,
    lifts,
    couples,
    spreads,
    lift_here,
    couple_here,
    spread_here,
    pair_sent,
    pair_got,
    select,
    diag_poles,
    in_poles,
    out_poles,
    up_sent,
    up_got,
    top,
    cross,
    down_sent,
    down_got,
    slab_sem,
    z_send,
    z_recv,
    in_send,
    in_recv,
    out_send,
    out_recv,
    tree_send,
    tree_recv,
    local_sem,
    store_sem,
    load_sem,
    pair_send,
    pair_recv,
):
    devices = groups * leaves
    chunks, width, cols = arrived.shape
    size = there_sent.shape[2]
    block = width // devices
    plane = leaves * block
    share = groups * block
    part_cols = cols // leaves
    group = lax.axis_index("grp")
    seat = lax.axis_index("leaf")

    def seats(step):
        def body(shift, carry):
            step(lax.rem(seat + shift, leaves))
            return carry

        lax.fori_loop(1, leaves, body, 0)

    def cols_of(chunk):
        return pl.ds(pl.multiple_of(chunk * cols, cols), cols)

    def below(apart):
        return lax.rem(group - apart + groups, groups)

    def above(apart):
        return lax.rem(group + apart, groups)

    def plane_rows(which):
        return pl.ds(pl.multiple_of(which * plane, plane), plane)

    def leaf_rows(which, other):
        return pl.ds(pl.multiple_of(which * plane + other * block, block), block)

    def part_rows(index):
        return pl.ds(pl.multiple_of(index * block, block), block)

    def share_part(other, apart):
        return pl.ds(pl.multiple_of(other * share + apart * block, block), block)

    barrier = greet(groups, leaves)

    def slab_load(chunk):
        return pltpu.make_async_copy(
            slab.at[:, cols_of(chunk)], slab_here.at[chunk], slab_sem.at[chunk]
        )

    def each(low, high, step):
        def body(index, carry):
            step(index)
            return carry

        lax.fori_loop(low, high, body, 0)

    each(0, chunks, lambda chunk: slab_load(chunk).start())

    pairs = [(diag, diag_here), (gen_in, in_here), (gen_out, out_here)]
    pairs += [(inner_lift, lifts), (inner_couple, couples), (inner_spread, spreads)]
    pairs += [(leaf_lift.at[0], lift_here), (leaf_couple.at[0], couple_here)]
    pairs += [(leaf_spread.at[0], spread_here)]
    loads = [
        pltpu.make_async_copy(source, target, load_sem.at[index])
        for index, (source, target) in enumerate(pairs)
    ]
    for load in loads:
        load.start()

    turned = marks[...].T
    row = lax.broadcasted_iota(jnp.int32, (size, plane), 0).astype(jnp.float32)
    lane = lax.broadcasted_iota(jnp.int32, (plane, size), 1).astype(jnp.float32)

    def along(role):
        return jnp.where(row == marks[role : role + 1, :], 1.0, 0.0).astype(jnp.bfloat16)

    def across(role):
        return jnp.where(lane == turned[:, role : role + 1], 1.0, 0.0).astype(jnp.bfloat16)

    for apart in range(1, groups):
        pack_at[0, apart - 1] = along(apart)
    pl.semaphore_wait(barrier, devices - 1)

    def z_copy(source, target, way, chunk, apart, device):
        return pltpu.make_async_remote_copy(
            src_ref=source,
            dst_ref=target,
            send_sem=z_send.at[way, chunk, apart - 1],
            recv_sem=z_recv.at[way, chunk, apart - 1],
            device_id=(device, seat),
            device_id_type=MESH,
        )

    def send_there(chunk, apart):
        return z_copy(
            there_sent.at[chunk, apart - 1],
            there_got.at[chunk, apart - 1],
            0,
            chunk,
            apart,
            below(apart),
        )

    def send_back(chunk, apart):
        return z_copy(
            back_sent.at[chunk, apart - 1],
            back_got.at[chunk, apart - 1],
            1,
            chunk,
            apart,
            above(apart),
        )

    def deliver(source, chunk, apart):
        target = arrived.at[chunk, share_part(seat, apart)]
        seats(
            lambda other: pltpu.make_async_remote_copy(
                src_ref=source(other),
                dst_ref=target,
                send_sem=in_send.at[apart, chunk],
                recv_sem=in_recv.at[apart, chunk],
                device_id=(group, other),
                device_id_type=MESH,
            ).start()
        )
        pltpu.make_async_copy(source(seat), target, local_sem.at[0, apart, chunk]).start()

    def send_in(chunk):
        slab_load(chunk).wait()

        def pack(apart):
            there_sent[chunk, apart - 1] = row_dot(
                pack_at[0, apart - 1], slab_here[chunk, plane_rows(below(apart)), :]
            ).astype(jnp.bfloat16)
            send_there(chunk, apart).start()

        each(1, groups, pack)
        deliver(lambda other: slab.at[leaf_rows(group, other), cols_of(chunk)], chunk, 0)

    def wait_bytes(buffer, chunk, rows, semaphore):
        part = buffer.at[chunk, pl.ds(0, rows)]
        pltpu.make_async_copy(part, part, semaphore).wait()

    def relay_there(chunk, apart):
        send_there(chunk, apart).wait_recv()
        relay_in[chunk, apart - 1] = row_dot(
            unpack_at[0, apart - 1], there_got[chunk, apart - 1]
        ).astype(jnp.bfloat16)
        deliver(lambda other: relay_in.at[chunk, apart - 1, part_rows(other)], chunk, apart)

    def send_out(chunk):
        def go(index):
            apart = lax.rem(index + 1, groups)
            target = relay_out.at[chunk, apart, part_rows(seat)]
            seats(
                lambda other: pltpu.make_async_remote_copy(
                    src_ref=staged.at[chunk, share_part(other, apart)],
                    dst_ref=target,
                    send_sem=out_send.at[apart, chunk],
                    recv_sem=out_recv.at[apart, chunk],
                    device_id=(group, other),
                    device_id_type=MESH,
                ).start()
            )
            pltpu.make_async_copy(
                staged.at[chunk, share_part(seat, apart)], target, local_sem.at[1, apart, chunk]
            ).start()

        each(0, groups, go)

    def wait_back(chunk, apart):
        wait_bytes(staged, chunk, (leaves - 1) * block, out_recv.at[apart, chunk])
        wait_bytes(staged, chunk, block, local_sem.at[1, apart, chunk])

    def relay_back(chunk, apart):
        wait_back(chunk, apart)
        back_sent[chunk, apart - 1] = row_dot(
            pack_at[1, apart - 1], relay_out[chunk, apart]
        ).astype(jnp.bfloat16)
        send_back(chunk, apart).start()

    def put(chunk, apart, rows):
        which = plane_rows(below(apart))
        kept = slab_here[chunk, which, :].astype(jnp.float32)
        out_here_rows[chunk, which, :] = (rows + gone[apart] * kept).astype(jnp.bfloat16)

    def stores(chunk):
        return pltpu.make_async_copy(
            out_here_rows.at[chunk], out.at[:, cols_of(chunk)], store_sem.at[chunk]
        )

    def settle(chunk, apart):
        if apart == 1:
            wait_back(chunk, 0)
            put(chunk, 0, relay_out[chunk, 0].astype(jnp.float32))

        send_back(chunk, apart).wait_recv()
        put(chunk, apart, row_dot(unpack_at[1, apart - 1], back_got[chunk, apart - 1]))
        if apart == groups - 1:
            stores(chunk).start()

    def tree_copy(source, target, chunk, stage, device):
        return pltpu.make_async_remote_copy(
            src_ref=source,
            dst_ref=target,
            send_sem=tree_send.at[stage, chunk],
            recv_sem=tree_recv.at[stage, chunk],
            device_id=device,
            device_id_type=MESH,
        )

    each(0, min(AHEAD, chunks), send_in)

    for apart in range(1, groups):
        unpack_at[0, apart - 1] = across(groups + apart)
        pack_at[1, apart - 1] = along(groups + apart)
        unpack_at[1, apart - 1] = across(apart)
    for apart in range(groups):
        gone[apart] = jnp.where(turned[:, apart : apart + 1] < 0.0, 1.0, 0.0)

    slot = lax.broadcasted_iota(jnp.int32, (1, width), 1)
    pole = order[...]
    apart = lax.rem(lax.div(pole, plane) - group + groups, groups)
    inner = lax.rem(pole, plane)
    moved = lax.div(inner, block) * share + apart * block + lax.rem(inner, block)
    key = jnp.where(slot < live[...], moved, -1)
    part = min(256, width)
    for start in range(0, width, part):
        pole = lax.broadcasted_iota(jnp.int32, (part, width), 0) + start
        select[start : start + part, :] = jnp.where(pole == key, 1.0, 0.0).astype(jnp.bfloat16)

    for load in loads:
        load.wait()

    def fold(index, carry):
        start = pl.multiple_of(index * part, part)
        rows = pl.ds(start, part)
        chosen = select[rows, :]
        out_poles[rows, :] = row_dot(chosen, out_here[...]).astype(jnp.bfloat16)
        in_poles[rows, :] = row_dot(chosen, in_here[...])
        return carry

    lax.fori_loop(0, width // part, fold, 0)
    gather = in_poles[...].T.astype(jnp.bfloat16)

    def fold_diag(index):
        rows = pl.ds(pl.multiple_of(index * part, part), part)
        half = row_dot(select[rows, :], diag_here[...]).astype(jnp.bfloat16)
        full = lax.dot_general(
            half, select[...], (((1,), (1,)), ((), ())), preferred_element_type=jnp.float32
        )
        diag_poles[rows, :] = full.astype(jnp.bfloat16)

    def seat_rows(other):
        return pl.ds(pl.multiple_of(other * part_cols, part_cols), part_cols)

    def wait_up(chunk, semaphore):
        most = up_got.at[chunk, pl.ds(0, leaves - 1)]
        pltpu.make_async_copy(most, most, semaphore).wait()

    def wait_top(chunk, semaphore):
        most = top.at[chunk, pl.ds(0, groups - 1)]
        pltpu.make_async_copy(most, most, semaphore).wait()

    def wait_down(chunk, semaphore):
        most = down_got.at[chunk, pl.ds(0, cols - part_cols)]
        pltpu.make_async_copy(most, most, semaphore).wait()

    def node(local):
        depth = local.bit_length() - 1
        return (groups + group) * (1 << depth) + (local - (1 << depth))

    def lift_of(local):
        return lifts[node(local) - 4]

    def couple_of(local):
        return couples[node(local) - 2]

    def spread_of(local):
        return spreads[node(local) - 4]

    def pair_copy(chunk):
        return pltpu.make_async_remote_copy(
            src_ref=pair_sent.at[chunk],
            dst_ref=pair_got.at[chunk],
            send_sem=pair_send.at[chunk],
            recv_sem=pair_recv.at[chunk],
            device_id=(group, seat + 1 - 2 * lax.rem(seat, 2)),
            device_id_type=MESH,
        )

    def first(chunk):
        def ready(apart):
            wait_bytes(arrived, chunk, (leaves - 1) * block, in_recv.at[apart, chunk])
            wait_bytes(arrived, chunk, block, local_sem.at[0, apart, chunk])

        each(0, groups, ready)
        skeleton = row_dot(gather, arrived[chunk]).T
        up_sent[chunk] = fine_times(lift_here[...], skeleton).astype(jnp.bfloat16)
        seats(
            lambda other: tree_copy(
                up_sent.at[chunk, seat_rows(other)], up_got.at[chunk, seat], chunk, 0, (group, other)
            ).start()
        )
        up_got[chunk, seat] = up_sent[chunk, seat_rows(seat), :]
        pair_sent[chunk] = fine_times(couple_here[...], skeleton).astype(jnp.bfloat16)
        pair_copy(chunk).start()

    def second(chunk):
        wait_up(chunk, tree_recv.at[0, chunk])
        skeletons = {}
        for index in range(leaves // 2):
            left = up_got[chunk, 2 * index].astype(jnp.float32)
            right = up_got[chunk, 2 * index + 1].astype(jnp.float32)
            skeletons[leaves // 2 + index] = (left + right).astype(jnp.bfloat16)
        for local in range(leaves - 1, 1, -1):
            cross[chunk, local ^ 1] = times(couple_of(local), skeletons[local])
            if local % 2 == 0:
                skeletons[local // 2] = (
                    times(lift_of(local), skeletons[local])
                    + times(lift_of(local + 1), skeletons[local + 1])
                ).astype(jnp.bfloat16)
        top[chunk, groups + group] = skeletons[1]

        def body(shift, carry):
            tree_copy(
                top.at[chunk, groups + group],
                top.at[chunk, groups + group],
                chunk,
                1,
                (lax.rem(group + shift, groups), seat),
            ).start()
            return carry

        lax.fori_loop(1, groups, body, 0)

    def third(chunk):
        wait_top(chunk, tree_recv.at[1, chunk])
        for index in range(groups - 1, 1, -1):
            top[chunk, index] = (
                times(lifts[2 * index - 4], top[chunk, 2 * index])
                + times(lifts[2 * index - 3], top[chunk, 2 * index + 1])
            ).astype(jnp.bfloat16)
        incoming = None
        for height in range(groups.bit_length() - 2, -1, -1):
            mine = lax.div(groups + group, 1 << height)
            other = mine + 1 - 2 * lax.rem(mine, 2)
            crossed = times(couples[other - 2], top[chunk, other])
            if incoming is not None:
                crossed = crossed + fine_times(spreads[mine - 4], incoming)
            incoming = crossed
        passed = {1: incoming}
        for local in range(2, leaves):
            passed[local] = (
                fine_times(spread_of(local), passed[local // 2]) + cross[chunk, local]
            )
        for index in range(leaves // 2):
            down_sent[chunk, index] = passed[leaves // 2 + index].astype(jnp.bfloat16)
        seats(
            lambda other: tree_copy(
                down_sent.at[chunk, lax.div(other, 2)],
                down_got.at[chunk, seat_rows(seat)],
                chunk,
                2,
                (group, other),
            ).start()
        )
        down_got[chunk, seat_rows(seat), :] = down_sent[chunk, lax.div(seat, 2)]

    def finish(chunk):
        wait_down(chunk, tree_recv.at[2, chunk])
        pair_copy(chunk).wait_recv()
        incoming = times(spread_here[...], down_got[chunk]) + pair_got[chunk].astype(jnp.float32)
        incoming = incoming.T.astype(jnp.bfloat16)

        def rows_done(index, carry):
            rows = pl.ds(pl.multiple_of(index * part, part), part)
            value = row_dot(diag_poles[rows, :], arrived[chunk]) + row_dot(
                out_poles[rows, :], incoming
            )
            staged[chunk, rows, :] = value.astype(jnp.bfloat16)
            return carry

        lax.fori_loop(0, width // part, rows_done, 0)
        send_out(chunk)

    stages = (send_in, relay_there, first, second, third, finish, relay_back, settle, fold_diag)

    events = []
    for stage in range(len(stages)):
        pieces = groups - 1 if stage in (1, 6, 7) else 1
        for piece in range(pieces):
            at = STARTS[stage] + piece * (PERIOD // pieces)
            events.append((at % PERIOD, ORDER.index(stage), stage, piece + 1, at // PERIOD))

    def period(now):
        for _, _, stage, apart, lag in sorted(events):
            chunk = now - lag
            lowest = AHEAD if stage == 0 else 0

            @pl.when((chunk >= lowest) & (chunk < (1 if stage == 8 else chunks)))
            def run():
                if stage == 8:
                    each(0, width // part, fold_diag)
                elif stage in (1, 6, 7):
                    stages[stage](chunk, apart)
                else:
                    stages[stage](chunk)

    each(0, max(event[-1] for event in events) + chunks, period)

    def drain(chunk):
        for apart in range(1, groups):
            send_there(chunk, apart).wait_send()
            send_back(chunk, apart).wait_send()
        for apart in range(groups):
            wait_bytes(arrived, chunk, (leaves - 1) * block, in_send.at[apart, chunk])
            wait_bytes(staged, chunk, (leaves - 1) * block, out_send.at[apart, chunk])
        wait_up(chunk, tree_send.at[0, chunk])
        wait_top(chunk, tree_send.at[1, chunk])
        wait_down(chunk, tree_send.at[2, chunk])
        pair_copy(chunk).wait_send()
        stores(chunk).wait()

    each(0, chunks, drain)


def fused(
    basis_slab,
    live_counts,
    pole_order,
    leaf_diag,
    leaf_in,
    leaf_out,
    leaf_lift,
    leaf_couple,
    leaf_spread,
    inner_lift,
    inner_couple,
    inner_spread,
):
    groups = lax.axis_size("grp")
    leaves = lax.axis_size("leaf")
    devices = groups * leaves
    width, slab_rows = basis_slab.shape
    block = width // devices
    plane = leaves * block
    rank = leaf_in.shape[1]
    cols = slab_rows // CHUNKS
    vmem = pl.BlockSpec(memory_space=pltpu.VMEM)
    smem = pl.BlockSpec(memory_space=pltpu.SMEM)
    anywhere = pl.BlockSpec(memory_space=pl.ANY)
    half = jnp.bfloat16
    sizes = tuple(plane * level // LEVELS[-1] for level in LEVELS)
    counts = live_counts.reshape(1, 1)
    lanes = 128
    marks, level = pl.pallas_call(
        functools.partial(census_kernel, groups, leaves, sizes),
        out_shape=[
            jax.ShapeDtypeStruct((2 * groups, plane), jnp.float32),
            jax.ShapeDtypeStruct((1, 1), jnp.int32),
        ],
        in_specs=[vmem] * 2,
        out_specs=[vmem, smem],
        scratch_shapes=[
            pltpu.VMEM((devices, width // lanes, lanes), jnp.float32),
            pltpu.SemaphoreType.DMA,
            pltpu.SemaphoreType.DMA,
        ],
        compiler_params=pltpu.CompilerParams(collective_id=0, has_side_effects=True),
    )(counts, pole_order)

    def main(index):
        size = sizes[index]
        away = groups - 1
        return pl.pallas_call(
            functools.partial(fused_kernel, groups, leaves),
            out_shape=jax.ShapeDtypeStruct((width, slab_rows), half),
            in_specs=[anywhere] + [vmem] * 3 + [anywhere] * 9,
            out_specs=anywhere,
            scratch_shapes=[
                pltpu.VMEM((CHUNKS, width, cols), half),
                pltpu.VMEM((2, away, size, plane), half),
                pltpu.VMEM((2, away, plane, size), half),
                pltpu.VMEM((groups, plane, 1), jnp.float32),
                pltpu.VMEM((CHUNKS, away, size, cols), half),
                pltpu.VMEM((CHUNKS, away, size, cols), half),
                pltpu.VMEM((CHUNKS, away, plane, cols), half),
                pltpu.VMEM((CHUNKS, width, cols), half),
                pltpu.VMEM((CHUNKS, width, cols), half),
                pltpu.VMEM((CHUNKS, groups, plane, cols), half),
                pltpu.VMEM((CHUNKS, away, size, cols), half),
                pltpu.VMEM((CHUNKS, away, size, cols), half),
                pltpu.VMEM((CHUNKS, width, cols), half),
                pltpu.VMEM((width, width), half),
                pltpu.VMEM((width, rank), half),
                pltpu.VMEM((width, rank), half),
                pltpu.VMEM(inner_lift.shape, half),
                pltpu.VMEM(inner_couple.shape, half),
                pltpu.VMEM(inner_spread.shape, half),
                pltpu.VMEM((rank, rank), half),
                pltpu.VMEM((rank, rank), half),
                pltpu.VMEM((rank, rank), half),
                pltpu.VMEM((CHUNKS, cols, rank), half),
                pltpu.VMEM((CHUNKS, cols, rank), half),
                pltpu.VMEM((width, width), half),
                pltpu.VMEM((width, width), half),
                pltpu.VMEM((width, rank), jnp.float32),
                pltpu.VMEM((width, rank), half),
                pltpu.VMEM((CHUNKS, cols, rank), half),
                pltpu.VMEM((CHUNKS, leaves, cols // leaves, rank), half),
                pltpu.VMEM((CHUNKS, 2 * groups, cols // leaves, rank), half),
                pltpu.VMEM((CHUNKS, leaves, cols // leaves, rank), jnp.float32),
                pltpu.VMEM((CHUNKS, leaves // 2, cols // leaves, rank), half),
                pltpu.VMEM((CHUNKS, cols, rank), half),
                pltpu.SemaphoreType.DMA((CHUNKS,)),
                pltpu.SemaphoreType.DMA((2, CHUNKS, away)),
                pltpu.SemaphoreType.DMA((2, CHUNKS, away)),
                pltpu.SemaphoreType.DMA((groups, CHUNKS)),
                pltpu.SemaphoreType.DMA((groups, CHUNKS)),
                pltpu.SemaphoreType.DMA((groups, CHUNKS)),
                pltpu.SemaphoreType.DMA((groups, CHUNKS)),
                pltpu.SemaphoreType.DMA((3, CHUNKS)),
                pltpu.SemaphoreType.DMA((3, CHUNKS)),
                pltpu.SemaphoreType.DMA((2, groups, CHUNKS)),
                pltpu.SemaphoreType.DMA((CHUNKS,)),
                pltpu.SemaphoreType.DMA((9,)),
                pltpu.SemaphoreType.DMA((CHUNKS,)),
                pltpu.SemaphoreType.DMA((CHUNKS,)),
            ],
            compiler_params=pltpu.CompilerParams(
                collective_id=1 + index, has_side_effects=True, vmem_limit_bytes=56 * 1024 * 1024
            ),
        )(
            basis_slab,
            counts,
            pole_order,
            marks,
            leaf_diag,
            leaf_in,
            leaf_out,
            leaf_lift,
            leaf_couple,
            leaf_spread,
            inner_lift,
            inner_couple,
            inner_spread,
        )

    branches = [functools.partial(main, index) for index in range(len(sizes))]
    return lax.switch(level[0, 0], branches)


def from_partner(block, axis, apart):
    count = lax.axis_size(axis)
    route = []
    for low in range(count):
        high = low | 1 << apart
        if high != low and high < count:
            route += [(low, high), (high, low)]
    return lax.ppermute(block, axis, route)


def transform(matrix, stacked):
    return jnp.dot(matrix.astype(jnp.float32), stacked, precision=lax.Precision.HIGHEST)


def local(
    basis_slab,
    live_counts,
    pole_order,
    leaf_diag,
    leaf_in,
    leaf_out,
    leaf_lift,
    leaf_couple,
    leaf_spread,
    inner_lift,
    inner_couple,
    inner_spread,
):
    groups = lax.axis_size("grp")
    leaves = lax.axis_size("leaf")
    devices = groups * leaves
    leaf_width = basis_slab.shape[0]
    slab_rows = basis_slab.shape[1]
    block_rows = leaf_width // devices
    levels = devices.bit_length() - 1
    leaf_bits = leaves.bit_length() - 1
    position = lax.axis_index("grp") * leaves + lax.axis_index("leaf")

    def redistribute(columns):
        arrived = lax.all_to_all(
            columns.reshape(devices, block_rows, slab_rows),
            ("grp", "leaf"),
            split_axis=0,
            concat_axis=0,
            tiled=True,
        )
        return arrived.reshape(leaf_width, slab_rows)

    def node_matrix(height, leaf_table, inner_table, offset):
        if height == 0:
            return leaf_table[0]
        own_node = jnp.right_shift(devices + position, height)
        return lax.dynamic_index_in_dim(inner_table, own_node - offset, 0, keepdims=False)

    leaf_rows = redistribute(basis_slab)
    slot_order = pole_order[0]
    live_count = live_counts[0]
    slots = jnp.take(leaf_rows, slot_order, axis=0)
    live_mask = jnp.arange(leaf_width, dtype=jnp.int32) < live_count
    masked = jnp.where(live_mask[:, None], slots, jnp.zeros_like(slots))
    skeleton = jnp.einsum("mk,mc->kc", leaf_in, masked, preferred_element_type=jnp.float32)
    crosses = []
    for height in range(leaf_bits):
        lifted = transform(node_matrix(height, leaf_lift, inner_lift, 4), skeleton)
        coupled = transform(node_matrix(height, leaf_couple, inner_couple, 2), skeleton)
        other_lift, other_cross = from_partner((lifted, coupled), "leaf", height)
        crosses.append(other_cross)
        skeleton = lifted + other_lift
    group_bits = groups.bit_length() - 1
    for height in range(leaf_bits, levels - 1):
        lifted = transform(node_matrix(height, leaf_lift, inner_lift, 4), skeleton)
        coupled = transform(node_matrix(height, leaf_couple, inner_couple, 2), skeleton)
        other_lift, other_cross = (
            from_partner(lifted.astype(jnp.bfloat16), "grp", height - leaf_bits).astype(
                lifted.dtype
            ),
            from_partner(coupled.astype(jnp.bfloat16), "grp", height - leaf_bits).astype(
                coupled.dtype
            ),
        )
        crosses.append(other_cross)
        skeleton = lifted + other_lift
    coupled = transform(node_matrix(levels - 1, leaf_couple, inner_couple, 2), skeleton)
    crosses.append(
        from_partner(coupled.astype(jnp.bfloat16), "grp", group_bits - 1).astype(coupled.dtype)
    )
    incoming = crosses[levels - 1]
    for height in range(levels - 2, -1, -1):
        incoming = (
            transform(node_matrix(height, leaf_spread, inner_spread, 4), incoming) + crosses[height]
        )
    incoming_b = incoming.astype(jnp.bfloat16)
    tile_rows = leaf_width // 8
    tile_count = live_count // tile_rows

    def one_tile(tile_index, merged_rows):
        row_start = tile_index * tile_rows
        diag_rows = lax.dynamic_slice_in_dim(leaf_diag, row_start, tile_rows, 0)
        out_rows = lax.dynamic_slice_in_dim(leaf_out, row_start, tile_rows, 0)
        value = jnp.dot(diag_rows, masked, preferred_element_type=jnp.float32) + jnp.dot(
            out_rows, incoming_b, preferred_element_type=jnp.float32
        )
        return lax.dynamic_update_slice_in_dim(merged_rows, value, row_start, 0)

    merged_rows = lax.fori_loop(
        0, tile_count, one_tile, jnp.zeros((leaf_width, slab_rows), jnp.float32)
    )
    updated = jnp.where(live_mask[:, None], merged_rows, slots.astype(jnp.float32)).astype(
        jnp.bfloat16
    )
    inverse = (
        jnp.zeros((leaf_width,), jnp.int32)
        .at[slot_order]
        .set(jnp.arange(leaf_width, dtype=jnp.int32))
    )
    restored = jnp.take(updated, inverse, axis=0)
    return redistribute(restored)


def solution(mesh):
    placed = (
        P(("grp", "leaf"), None),
        P(("grp", "leaf")),
        P(("grp", "leaf"), None),
        P(("grp", "leaf"), None),
        P(("grp", "leaf"), None),
        P(("grp", "leaf"), None),
        P(("grp", "leaf"), None, None),
        P(("grp", "leaf"), None, None),
        P(("grp", "leaf"), None, None),
        P(),
        P(),
        P(),
    )

    def step(basis_slab, *rest):
        devices = mesh.shape["grp"] * mesh.shape["leaf"]
        block_rows = basis_slab.shape[0] // devices
        whole_tiles = (
            block_rows % 16 == 0
            and 128 % block_rows == 0
            and mesh.shape["leaf"] % (128 // block_rows) == 0
            and basis_slab.shape[1] % (128 * CHUNKS) == 0
            and basis_slab.shape[1] % (16 * CHUNKS * mesh.shape["leaf"]) == 0
        )
        return (fused if whole_tiles else local)(basis_slab, *rest)

    return jax.shard_map(
        step, mesh=mesh, in_specs=placed, out_specs=P(("grp", "leaf"), None), check_vma=False
    )
```

```python
import functools

import jax
import jax.numpy as jnp
from jax import lax
from jax.experimental import pallas as pl
from jax.experimental.pallas import tpu as pltpu
from jax.sharding import PartitionSpec as P

MESH = pl.DeviceIdType.MESH
PERIOD = 12
COARSE = (4, 2, (-9, 3, 16, 27, 39, 53, 65, 96, 2), (8, 4, 7, 3, 2, 5, 6, 1, 0))
FINE = (8, 4, (-9, 11, 35, 51, 70, 85, 98, 121, 14), (4, 8, 7, 2, 5, 3, 0, 1, 6))
LEVELS = ((9, COARSE), (10, COARSE), (11, FINE), (12, FINE), (13, FINE), (16, FINE))
MOST_CHUNKS = max(plan[0] for _, plan in LEVELS)


def row_dot(a, b):
    return jnp.dot(a, b, preferred_element_type=jnp.float32)


def times(matrix, rows):
    return lax.dot_general(
        rows, matrix, (((1,), (1,)), ((), ())), preferred_element_type=jnp.float32
    )


def fine_times(matrix, rows):
    high = rows.astype(jnp.bfloat16)
    low = (rows - high.astype(jnp.float32)).astype(jnp.bfloat16)
    return times(matrix, high) + times(matrix, low)


def greet(groups, leaves):
    devices = groups * leaves
    me = lax.axis_index("grp") * leaves + lax.axis_index("leaf")
    barrier = pltpu.get_barrier_semaphore()

    def body(shift, carry):
        device = lax.rem(me + shift, devices)
        pl.semaphore_signal(
            barrier,
            inc=1,
            device_id=(lax.div(device, leaves), lax.rem(device, leaves)),
            device_id_type=MESH,
        )
        return carry

    lax.fori_loop(1, devices, body, 0)
    return barrier


def census_kernel(groups, leaves, sizes, live, order, marks, level, table, send, recv):
    devices, tall, lanes = table.shape
    width = order.shape[1]
    block = width // devices
    plane = leaves * block
    per = lanes // block
    group = lax.axis_index("grp")
    seat = lax.axis_index("leaf")
    me = group * leaves + seat
    barrier = greet(groups, leaves)

    slot = lax.broadcasted_iota(jnp.int32, (1, width), 1)
    key = jnp.where(slot < live[...], order[...], -1)
    high = jnp.right_shift(key, lanes.bit_length() - 1)
    low = jnp.bitwise_and(key, lanes - 1)
    high_is = jnp.where(lax.broadcasted_iota(jnp.int32, (tall, width), 0) == high, 1.0, 0.0)
    low_is = jnp.where(lax.broadcasted_iota(jnp.int32, (lanes, width), 0) == low, 1.0, 0.0)
    table[me] = times(low_is.astype(jnp.bfloat16), high_is.astype(jnp.bfloat16))

    pl.semaphore_wait(barrier, devices - 1)

    def body(shift, carry):
        device = lax.rem(me + shift, devices)
        pltpu.make_async_remote_copy(
            src_ref=table.at[me],
            dst_ref=table.at[me],
            send_sem=send,
            recv_sem=recv,
            device_id=(lax.div(device, leaves), lax.rem(device, leaves)),
            device_id_type=MESH,
        ).start()
        return carry

    lax.fori_loop(1, devices, body, 0)
    lane = lax.broadcasted_iota(jnp.int32, (lanes, lanes), 0)
    bucket = jnp.where(
        lax.div(lane, block) == lax.broadcasted_iota(jnp.int32, (lanes, lanes), 1), 1.0, 0.0
    ).astype(jnp.bfloat16)
    lane = lax.broadcasted_iota(jnp.int32, (lanes, plane), 0)
    row = lax.broadcasted_iota(jnp.int32, (lanes, plane), 1)
    spread = jnp.where(
        lane == lax.rem(seat, per) * block + lax.rem(row, block), 1.0, 0.0
    ).astype(jnp.bfloat16)
    before = jnp.where(
        lax.broadcasted_iota(jnp.int32, (plane, plane), 0)
        < lax.broadcasted_iota(jnp.int32, (plane, plane), 1),
        1.0,
        0.0,
    ).astype(jnp.bfloat16)
    few = table.at[pl.ds(0, devices - 1)]
    pltpu.make_async_copy(few, few, recv).wait()

    owner = lax.broadcasted_iota(jnp.int32, (tall, lanes), 0) * per + lax.broadcasted_iota(
        jnp.int32, (tall, lanes), 1
    )
    inside = lax.broadcasted_iota(jnp.int32, (tall, lanes), 1) < per
    most = jnp.zeros((tall, lanes), jnp.float32)
    for target in range(groups):
        total = jnp.sum(table[target * leaves : (target + 1) * leaves], axis=0)
        counts = row_dot(total.astype(jnp.bfloat16), bucket)
        away = inside & (lax.div(owner, leaves) != target)
        most = jnp.maximum(most, jnp.where(away, counts, 0.0))
    largest = jnp.max(most)
    pick = jnp.int32(0)
    for size in sizes[:-1]:
        pick = pick + jnp.where(largest > size, 1, 0).astype(jnp.int32)
    level[0, 0] = pick

    def strip(first_leaf, device):
        rows = table[pl.ds(first_leaf, leaves)]
        at = lax.broadcasted_iota(jnp.int32, rows.shape, 1)
        return jnp.sum(jnp.where(at == lax.div(device, per), rows, 0.0), axis=1)

    strips = []
    for apart in range(groups):
        strips.append(strip(lax.rem(group - apart + groups, groups) * leaves, me))
    for apart in range(groups):
        other = lax.rem(group + apart, groups)
        strips.append(strip(group * leaves, other * leaves + seat))
    wide = row_dot(jnp.concatenate(strips, axis=0).astype(jnp.bfloat16), spread)
    leaf = lax.rem(lax.broadcasted_iota(jnp.int32, wide.shape, 0), leaves)
    here = leaf == lax.div(lax.broadcasted_iota(jnp.int32, wide.shape, 1), block)
    flags = jnp.sum(jnp.where(here, wide, 0.0).reshape(2 * groups, leaves, plane), axis=1)
    ranks = row_dot(flags.astype(jnp.bfloat16), before)
    marks[...] = jnp.where(flags > 0.5, ranks, -1.0)
    pltpu.make_async_copy(few, few, send).wait()


def fused_kernel(
    groups,
    leaves,
    plan,
    slab,
    live,
    order,
    marks,
    diag,
    gen_in,
    gen_out,
    leaf_lift,
    leaf_couple,
    leaf_spread,
    inner_lift,
    inner_couple,
    inner_spread,
    out,
    slab_here,
    pack_at,
    unpack_at,
    gone,
    there_sent,
    there_got,
    relay_in,
    arrived,
    staged,
    relay_out,
    back_sent,
    back_got,
    out_here_rows,
    diag_here,
    in_here,
    out_here,
    lifts,
    couples,
    spreads,
    lift_here,
    couple_here,
    spread_here,
    pair_sent,
    pair_got,
    select,
    diag_poles,
    in_poles,
    out_poles,
    up_sent,
    up_got,
    top,
    cross,
    down_sent,
    down_got,
    slab_sem,
    z_send,
    z_recv,
    in_send,
    in_recv,
    out_send,
    out_recv,
    tree_send,
    tree_recv,
    local_sem,
    store_sem,
    load_sem,
    pair_send,
    pair_recv,
):
    devices = groups * leaves
    chunks, width, cols = arrived.shape
    _, ahead, starts, ranks = plan
    size = there_sent.shape[2]
    block = width // devices
    plane = leaves * block
    share = groups * block
    part_cols = cols // leaves
    group = lax.axis_index("grp")
    seat = lax.axis_index("leaf")

    def seats(step):
        def body(shift, carry):
            step(lax.rem(seat + shift, leaves))
            return carry

        lax.fori_loop(1, leaves, body, 0)

    def cols_of(chunk):
        return pl.ds(pl.multiple_of(chunk * cols, cols), cols)

    def below(apart):
        return lax.rem(group - apart + groups, groups)

    def above(apart):
        return lax.rem(group + apart, groups)

    def plane_rows(which):
        return pl.ds(pl.multiple_of(which * plane, plane), plane)

    def leaf_rows(which, other):
        return pl.ds(pl.multiple_of(which * plane + other * block, block), block)

    def part_rows(index):
        return pl.ds(pl.multiple_of(index * block, block), block)

    def share_part(other, apart):
        return pl.ds(pl.multiple_of(other * share + apart * block, block), block)

    barrier = greet(groups, leaves)

    def slab_load(chunk):
        return pltpu.make_async_copy(
            slab.at[:, cols_of(chunk)], slab_here.at[chunk], slab_sem.at[chunk]
        )

    def each(low, high, step):
        def body(index, carry):
            step(index)
            return carry

        lax.fori_loop(low, high, body, 0)

    each(0, chunks, lambda chunk: slab_load(chunk).start())

    pairs = [(diag, diag_here), (gen_in, in_here), (gen_out, out_here)]
    pairs += [(inner_lift, lifts), (inner_couple, couples), (inner_spread, spreads)]
    pairs += [(leaf_lift.at[0], lift_here), (leaf_couple.at[0], couple_here)]
    pairs += [(leaf_spread.at[0], spread_here)]
    loads = [
        pltpu.make_async_copy(source, target, load_sem.at[index])
        for index, (source, target) in enumerate(pairs)
    ]
    for load in loads:
        load.start()

    turned = marks[...].T
    row = lax.broadcasted_iota(jnp.int32, (size, plane), 0).astype(jnp.float32)
    lane = lax.broadcasted_iota(jnp.int32, (plane, size), 1).astype(jnp.float32)

    def along(role):
        return jnp.where(row == marks[role : role + 1, :], 1.0, 0.0).astype(jnp.bfloat16)

    def across(role):
        return jnp.where(lane == turned[:, role : role + 1], 1.0, 0.0).astype(jnp.bfloat16)

    for apart in range(1, groups):
        pack_at[0, apart - 1] = along(apart)
    pl.semaphore_wait(barrier, devices - 1)

    def z_copy(source, target, way, chunk, apart, device):
        return pltpu.make_async_remote_copy(
            src_ref=source,
            dst_ref=target,
            send_sem=z_send.at[way, chunk, apart - 1],
            recv_sem=z_recv.at[way, chunk, apart - 1],
            device_id=(device, seat),
            device_id_type=MESH,
        )

    def send_there(chunk, apart):
        return z_copy(
            there_sent.at[chunk, apart - 1],
            there_got.at[chunk, apart - 1],
            0,
            chunk,
            apart,
            below(apart),
        )

    def send_back(chunk, apart):
        return z_copy(
            back_sent.at[chunk, apart - 1],
            back_got.at[chunk, apart - 1],
            1,
            chunk,
            apart,
            above(apart),
        )

    def deliver(source, chunk, apart):
        target = arrived.at[chunk, share_part(seat, apart)]
        seats(
            lambda other: pltpu.make_async_remote_copy(
                src_ref=source(other),
                dst_ref=target,
                send_sem=in_send.at[apart, chunk],
                recv_sem=in_recv.at[apart, chunk],
                device_id=(group, other),
                device_id_type=MESH,
            ).start()
        )
        pltpu.make_async_copy(source(seat), target, local_sem.at[0, apart, chunk]).start()

    def send_in(chunk):
        slab_load(chunk).wait()

        def pack(apart):
            there_sent[chunk, apart - 1] = row_dot(
                pack_at[0, apart - 1], slab_here[chunk, plane_rows(below(apart)), :]
            ).astype(jnp.bfloat16)
            send_there(chunk, apart).start()

        each(1, groups, pack)
        deliver(lambda other: slab.at[leaf_rows(group, other), cols_of(chunk)], chunk, 0)

    def wait_bytes(buffer, chunk, rows, semaphore):
        part = buffer.at[chunk, pl.ds(0, rows)]
        pltpu.make_async_copy(part, part, semaphore).wait()

    def relay_there(chunk, apart):
        send_there(chunk, apart).wait_recv()
        relay_in[chunk, apart - 1] = row_dot(
            unpack_at[0, apart - 1], there_got[chunk, apart - 1]
        ).astype(jnp.bfloat16)
        deliver(lambda other: relay_in.at[chunk, apart - 1, part_rows(other)], chunk, apart)

    def send_out(chunk):
        def go(index):
            apart = lax.rem(index + 1, groups)
            target = relay_out.at[chunk, apart, part_rows(seat)]
            seats(
                lambda other: pltpu.make_async_remote_copy(
                    src_ref=staged.at[chunk, share_part(other, apart)],
                    dst_ref=target,
                    send_sem=out_send.at[apart, chunk],
                    recv_sem=out_recv.at[apart, chunk],
                    device_id=(group, other),
                    device_id_type=MESH,
                ).start()
            )
            pltpu.make_async_copy(
                staged.at[chunk, share_part(seat, apart)], target, local_sem.at[1, apart, chunk]
            ).start()

        each(0, groups, go)

    def wait_back(chunk, apart):
        wait_bytes(staged, chunk, (leaves - 1) * block, out_recv.at[apart, chunk])
        wait_bytes(staged, chunk, block, local_sem.at[1, apart, chunk])

    def relay_back(chunk, apart):
        wait_back(chunk, apart)
        back_sent[chunk, apart - 1] = row_dot(
            pack_at[1, apart - 1], relay_out[chunk, apart]
        ).astype(jnp.bfloat16)
        send_back(chunk, apart).start()

    def put(chunk, apart, rows):
        which = plane_rows(below(apart))
        kept = slab_here[chunk, which, :].astype(jnp.float32)
        out_here_rows[chunk, which, :] = (rows + gone[apart] * kept).astype(jnp.bfloat16)

    def stores(chunk):
        return pltpu.make_async_copy(
            out_here_rows.at[chunk], out.at[:, cols_of(chunk)], store_sem.at[chunk]
        )

    def settle(chunk, apart):
        if apart == 1:
            wait_back(chunk, 0)
            put(chunk, 0, relay_out[chunk, 0].astype(jnp.float32))

        send_back(chunk, apart).wait_recv()
        put(chunk, apart, row_dot(unpack_at[1, apart - 1], back_got[chunk, apart - 1]))
        if apart == groups - 1:
            stores(chunk).start()

    def tree_copy(source, target, chunk, stage, device):
        return pltpu.make_async_remote_copy(
            src_ref=source,
            dst_ref=target,
            send_sem=tree_send.at[stage, chunk],
            recv_sem=tree_recv.at[stage, chunk],
            device_id=device,
            device_id_type=MESH,
        )

    each(0, min(ahead, chunks), send_in)

    for apart in range(1, groups):
        unpack_at[0, apart - 1] = across(groups + apart)
        pack_at[1, apart - 1] = along(groups + apart)
        unpack_at[1, apart - 1] = across(apart)
    for apart in range(groups):
        gone[apart] = jnp.where(turned[:, apart : apart + 1] < 0.0, 1.0, 0.0)

    slot = lax.broadcasted_iota(jnp.int32, (1, width), 1)
    pole = order[...]
    apart = lax.rem(lax.div(pole, plane) - group + groups, groups)
    inner = lax.rem(pole, plane)
    moved = lax.div(inner, block) * share + apart * block + lax.rem(inner, block)
    key = jnp.where(slot < live[...], moved, -1)
    part = min(256, width)
    for start in range(0, width, part):
        pole = lax.broadcasted_iota(jnp.int32, (part, width), 0) + start
        select[start : start + part, :] = jnp.where(pole == key, 1.0, 0.0).astype(jnp.bfloat16)

    for load in loads:
        load.wait()

    def fold(index, carry):
        start = pl.multiple_of(index * part, part)
        rows = pl.ds(start, part)
        chosen = select[rows, :]
        out_poles[rows, :] = row_dot(chosen, out_here[...]).astype(jnp.bfloat16)
        in_poles[rows, :] = row_dot(chosen, in_here[...])
        return carry

    lax.fori_loop(0, width // part, fold, 0)
    gather = in_poles[...].T.astype(jnp.bfloat16)

    def fold_diag(index):
        rows = pl.ds(pl.multiple_of(index * part, part), part)
        half = row_dot(select[rows, :], diag_here[...]).astype(jnp.bfloat16)
        full = lax.dot_general(
            half, select[...], (((1,), (1,)), ((), ())), preferred_element_type=jnp.float32
        )
        diag_poles[rows, :] = full.astype(jnp.bfloat16)

    def seat_rows(other):
        return pl.ds(pl.multiple_of(other * part_cols, part_cols), part_cols)

    def wait_up(chunk, semaphore):
        most = up_got.at[chunk, pl.ds(0, leaves - 1)]
        pltpu.make_async_copy(most, most, semaphore).wait()

    def wait_top(chunk, semaphore):
        most = top.at[chunk, pl.ds(0, groups - 1)]
        pltpu.make_async_copy(most, most, semaphore).wait()

    def wait_down(chunk, semaphore):
        most = down_got.at[chunk, pl.ds(0, cols - part_cols)]
        pltpu.make_async_copy(most, most, semaphore).wait()

    def node(local):
        depth = local.bit_length() - 1
        return (groups + group) * (1 << depth) + (local - (1 << depth))

    def lift_of(local):
        return lifts[node(local) - 4]

    def couple_of(local):
        return couples[node(local) - 2]

    def spread_of(local):
        return spreads[node(local) - 4]

    def pair_copy(chunk):
        return pltpu.make_async_remote_copy(
            src_ref=pair_sent.at[chunk],
            dst_ref=pair_got.at[chunk],
            send_sem=pair_send.at[chunk],
            recv_sem=pair_recv.at[chunk],
            device_id=(group, seat + 1 - 2 * lax.rem(seat, 2)),
            device_id_type=MESH,
        )

    def first(chunk):
        def ready(apart):
            wait_bytes(arrived, chunk, (leaves - 1) * block, in_recv.at[apart, chunk])
            wait_bytes(arrived, chunk, block, local_sem.at[0, apart, chunk])

        each(0, groups, ready)
        skeleton = row_dot(gather, arrived[chunk]).T
        up_sent[chunk] = fine_times(lift_here[...], skeleton).astype(jnp.bfloat16)
        seats(
            lambda other: tree_copy(
                up_sent.at[chunk, seat_rows(other)], up_got.at[chunk, seat], chunk, 0, (group, other)
            ).start()
        )
        up_got[chunk, seat] = up_sent[chunk, seat_rows(seat), :]
        pair_sent[chunk] = fine_times(couple_here[...], skeleton).astype(jnp.bfloat16)
        pair_copy(chunk).start()

    def second(chunk):
        wait_up(chunk, tree_recv.at[0, chunk])
        skeletons = {}
        for index in range(leaves // 2):
            left = up_got[chunk, 2 * index].astype(jnp.float32)
            right = up_got[chunk, 2 * index + 1].astype(jnp.float32)
            skeletons[leaves // 2 + index] = (left + right).astype(jnp.bfloat16)
        for local in range(leaves - 1, 1, -1):
            cross[chunk, local ^ 1] = times(couple_of(local), skeletons[local])
            if local % 2 == 0:
                skeletons[local // 2] = (
                    times(lift_of(local), skeletons[local])
                    + times(lift_of(local + 1), skeletons[local + 1])
                ).astype(jnp.bfloat16)
        top[chunk, groups + group] = skeletons[1]

        def body(shift, carry):
            tree_copy(
                top.at[chunk, groups + group],
                top.at[chunk, groups + group],
                chunk,
                1,
                (lax.rem(group + shift, groups), seat),
            ).start()
            return carry

        lax.fori_loop(1, groups, body, 0)

    def third(chunk):
        wait_top(chunk, tree_recv.at[1, chunk])
        for index in range(groups - 1, 1, -1):
            top[chunk, index] = (
                times(lifts[2 * index - 4], top[chunk, 2 * index])
                + times(lifts[2 * index - 3], top[chunk, 2 * index + 1])
            ).astype(jnp.bfloat16)
        incoming = None
        for height in range(groups.bit_length() - 2, -1, -1):
            mine = lax.div(groups + group, 1 << height)
            other = mine + 1 - 2 * lax.rem(mine, 2)
            crossed = times(couples[other - 2], top[chunk, other])
            if incoming is not None:
                crossed = crossed + fine_times(spreads[mine - 4], incoming)
            incoming = crossed
        passed = {1: incoming}
        for local in range(2, leaves):
            passed[local] = (
                fine_times(spread_of(local), passed[local // 2]) + cross[chunk, local]
            )
        for index in range(leaves // 2):
            down_sent[chunk, index] = passed[leaves // 2 + index].astype(jnp.bfloat16)
        seats(
            lambda other: tree_copy(
                down_sent.at[chunk, lax.div(other, 2)],
                down_got.at[chunk, seat_rows(seat)],
                chunk,
                2,
                (group, other),
            ).start()
        )
        down_got[chunk, seat_rows(seat), :] = down_sent[chunk, lax.div(seat, 2)]

    def finish(chunk):
        wait_down(chunk, tree_recv.at[2, chunk])
        pair_copy(chunk).wait_recv()
        incoming = times(spread_here[...], down_got[chunk]) + pair_got[chunk].astype(jnp.float32)
        incoming = incoming.T.astype(jnp.bfloat16)

        def rows_done(index, carry):
            rows = pl.ds(pl.multiple_of(index * part, part), part)
            value = row_dot(diag_poles[rows, :], arrived[chunk]) + row_dot(
                out_poles[rows, :], incoming
            )
            staged[chunk, rows, :] = value.astype(jnp.bfloat16)
            return carry

        lax.fori_loop(0, width // part, rows_done, 0)
        send_out(chunk)

    stages = (send_in, relay_there, first, second, third, finish, relay_back, settle, fold_diag)

    events = []
    for stage in range(len(stages)):
        pieces = groups - 1 if stage in (1, 6, 7) else 1
        for piece in range(pieces):
            at = starts[stage] + piece * (PERIOD // pieces)
            events.append((at % PERIOD, ranks.index(stage), stage, piece + 1, at // PERIOD))

    def period(now):
        for _, _, stage, apart, lag in sorted(events):
            chunk = now - lag
            lowest = ahead if stage == 0 else 0

            @pl.when((chunk >= lowest) & (chunk < (1 if stage == 8 else chunks)))
            def run():
                if stage == 8:
                    each(0, width // part, fold_diag)
                elif stage in (1, 6, 7):
                    stages[stage](chunk, apart)
                else:
                    stages[stage](chunk)

    each(0, max(event[-1] for event in events) + chunks, period)

    def drain(chunk):
        for apart in range(1, groups):
            send_there(chunk, apart).wait_send()
            send_back(chunk, apart).wait_send()
        for apart in range(groups):
            wait_bytes(arrived, chunk, (leaves - 1) * block, in_send.at[apart, chunk])
            wait_bytes(staged, chunk, (leaves - 1) * block, out_send.at[apart, chunk])
        wait_up(chunk, tree_send.at[0, chunk])
        wait_top(chunk, tree_send.at[1, chunk])
        wait_down(chunk, tree_send.at[2, chunk])
        pair_copy(chunk).wait_send()
        stores(chunk).wait()

    each(0, chunks, drain)


def fused(
    basis_slab,
    live_counts,
    pole_order,
    leaf_diag,
    leaf_in,
    leaf_out,
    leaf_lift,
    leaf_couple,
    leaf_spread,
    inner_lift,
    inner_couple,
    inner_spread,
):
    groups = lax.axis_size("grp")
    leaves = lax.axis_size("leaf")
    devices = groups * leaves
    width, slab_rows = basis_slab.shape
    block = width // devices
    plane = leaves * block
    rank = leaf_in.shape[1]
    vmem = pl.BlockSpec(memory_space=pltpu.VMEM)
    smem = pl.BlockSpec(memory_space=pltpu.SMEM)
    anywhere = pl.BlockSpec(memory_space=pl.ANY)
    half = jnp.bfloat16
    sizes = tuple(plane * level // LEVELS[-1][0] for level, _ in LEVELS)
    counts = live_counts.reshape(1, 1)
    lanes = 128
    marks, level = pl.pallas_call(
        functools.partial(census_kernel, groups, leaves, sizes),
        out_shape=[
            jax.ShapeDtypeStruct((2 * groups, plane), jnp.float32),
            jax.ShapeDtypeStruct((1, 1), jnp.int32),
        ],
        in_specs=[vmem] * 2,
        out_specs=[vmem, smem],
        scratch_shapes=[
            pltpu.VMEM((devices, width // lanes, lanes), jnp.float32),
            pltpu.SemaphoreType.DMA,
            pltpu.SemaphoreType.DMA,
        ],
        compiler_params=pltpu.CompilerParams(collective_id=0, has_side_effects=True),
    )(counts, pole_order)

    def main(index):
        size = sizes[index]
        plan = LEVELS[index][1]
        chunks = plan[0]
        cols = slab_rows // chunks
        away = groups - 1
        return pl.pallas_call(
            functools.partial(fused_kernel, groups, leaves, plan),
            out_shape=jax.ShapeDtypeStruct((width, slab_rows), half),
            in_specs=[anywhere] + [vmem] * 3 + [anywhere] * 9,
            out_specs=anywhere,
            scratch_shapes=[
                pltpu.VMEM((chunks, width, cols), half),
                pltpu.VMEM((2, away, size, plane), half),
                pltpu.VMEM((2, away, plane, size), half),
                pltpu.VMEM((groups, plane, 1), jnp.float32),
                pltpu.VMEM((chunks, away, size, cols), half),
                pltpu.VMEM((chunks, away, size, cols), half),
                pltpu.VMEM((chunks, away, plane, cols), half),
                pltpu.VMEM((chunks, width, cols), half),
                pltpu.VMEM((chunks, width, cols), half),
                pltpu.VMEM((chunks, groups, plane, cols), half),
                pltpu.VMEM((chunks, away, size, cols), half),
                pltpu.VMEM((chunks, away, size, cols), half),
                pltpu.VMEM((chunks, width, cols), half),
                pltpu.VMEM((width, width), half),
                pltpu.VMEM((width, rank), half),
                pltpu.VMEM((width, rank), half),
                pltpu.VMEM(inner_lift.shape, half),
                pltpu.VMEM(inner_couple.shape, half),
                pltpu.VMEM(inner_spread.shape, half),
                pltpu.VMEM((rank, rank), half),
                pltpu.VMEM((rank, rank), half),
                pltpu.VMEM((rank, rank), half),
                pltpu.VMEM((chunks, cols, rank), half),
                pltpu.VMEM((chunks, cols, rank), half),
                pltpu.VMEM((width, width), half),
                pltpu.VMEM((width, width), half),
                pltpu.VMEM((width, rank), jnp.float32),
                pltpu.VMEM((width, rank), half),
                pltpu.VMEM((chunks, cols, rank), half),
                pltpu.VMEM((chunks, leaves, cols // leaves, rank), half),
                pltpu.VMEM((chunks, 2 * groups, cols // leaves, rank), half),
                pltpu.VMEM((chunks, leaves, cols // leaves, rank), jnp.float32),
                pltpu.VMEM((chunks, leaves // 2, cols // leaves, rank), half),
                pltpu.VMEM((chunks, cols, rank), half),
                pltpu.SemaphoreType.DMA((chunks,)),
                pltpu.SemaphoreType.DMA((2, chunks, away)),
                pltpu.SemaphoreType.DMA((2, chunks, away)),
                pltpu.SemaphoreType.DMA((groups, chunks)),
                pltpu.SemaphoreType.DMA((groups, chunks)),
                pltpu.SemaphoreType.DMA((groups, chunks)),
                pltpu.SemaphoreType.DMA((groups, chunks)),
                pltpu.SemaphoreType.DMA((3, chunks)),
                pltpu.SemaphoreType.DMA((3, chunks)),
                pltpu.SemaphoreType.DMA((2, groups, chunks)),
                pltpu.SemaphoreType.DMA((chunks,)),
                pltpu.SemaphoreType.DMA((9,)),
                pltpu.SemaphoreType.DMA((chunks,)),
                pltpu.SemaphoreType.DMA((chunks,)),
            ],
            compiler_params=pltpu.CompilerParams(
                collective_id=1 + index, has_side_effects=True, vmem_limit_bytes=56 * 1024 * 1024
            ),
        )(
            basis_slab,
            counts,
            pole_order,
            marks,
            leaf_diag,
            leaf_in,
            leaf_out,
            leaf_lift,
            leaf_couple,
            leaf_spread,
            inner_lift,
            inner_couple,
            inner_spread,
        )

    branches = [functools.partial(main, index) for index in range(len(sizes))]
    return lax.switch(level[0, 0], branches)


def from_partner(block, axis, apart):
    count = lax.axis_size(axis)
    route = []
    for low in range(count):
        high = low | 1 << apart
        if high != low and high < count:
            route += [(low, high), (high, low)]
    return lax.ppermute(block, axis, route)


def transform(matrix, stacked):
    return jnp.dot(matrix.astype(jnp.float32), stacked, precision=lax.Precision.HIGHEST)


def local(
    basis_slab,
    live_counts,
    pole_order,
    leaf_diag,
    leaf_in,
    leaf_out,
    leaf_lift,
    leaf_couple,
    leaf_spread,
    inner_lift,
    inner_couple,
    inner_spread,
):
    groups = lax.axis_size("grp")
    leaves = lax.axis_size("leaf")
    devices = groups * leaves
    leaf_width = basis_slab.shape[0]
    slab_rows = basis_slab.shape[1]
    block_rows = leaf_width // devices
    levels = devices.bit_length() - 1
    leaf_bits = leaves.bit_length() - 1
    position = lax.axis_index("grp") * leaves + lax.axis_index("leaf")

    def redistribute(columns):
        arrived = lax.all_to_all(
            columns.reshape(devices, block_rows, slab_rows),
            ("grp", "leaf"),
            split_axis=0,
            concat_axis=0,
            tiled=True,
        )
        return arrived.reshape(leaf_width, slab_rows)

    def node_matrix(height, leaf_table, inner_table, offset):
        if height == 0:
            return leaf_table[0]
        own_node = jnp.right_shift(devices + position, height)
        return lax.dynamic_index_in_dim(inner_table, own_node - offset, 0, keepdims=False)

    leaf_rows = redistribute(basis_slab)
    slot_order = pole_order[0]
    live_count = live_counts[0]
    slots = jnp.take(leaf_rows, slot_order, axis=0)
    live_mask = jnp.arange(leaf_width, dtype=jnp.int32) < live_count
    masked = jnp.where(live_mask[:, None], slots, jnp.zeros_like(slots))
    skeleton = jnp.einsum("mk,mc->kc", leaf_in, masked, preferred_element_type=jnp.float32)
    crosses = []
    for height in range(leaf_bits):
        lifted = transform(node_matrix(height, leaf_lift, inner_lift, 4), skeleton)
        coupled = transform(node_matrix(height, leaf_couple, inner_couple, 2), skeleton)
        other_lift, other_cross = from_partner((lifted, coupled), "leaf", height)
        crosses.append(other_cross)
        skeleton = lifted + other_lift
    group_bits = groups.bit_length() - 1
    for height in range(leaf_bits, levels - 1):
        lifted = transform(node_matrix(height, leaf_lift, inner_lift, 4), skeleton)
        coupled = transform(node_matrix(height, leaf_couple, inner_couple, 2), skeleton)
        other_lift, other_cross = (
            from_partner(lifted.astype(jnp.bfloat16), "grp", height - leaf_bits).astype(
                lifted.dtype
            ),
            from_partner(coupled.astype(jnp.bfloat16), "grp", height - leaf_bits).astype(
                coupled.dtype
            ),
        )
        crosses.append(other_cross)
        skeleton = lifted + other_lift
    coupled = transform(node_matrix(levels - 1, leaf_couple, inner_couple, 2), skeleton)
    crosses.append(
        from_partner(coupled.astype(jnp.bfloat16), "grp", group_bits - 1).astype(coupled.dtype)
    )
    incoming = crosses[levels - 1]
    for height in range(levels - 2, -1, -1):
        incoming = (
            transform(node_matrix(height, leaf_spread, inner_spread, 4), incoming) + crosses[height]
        )
    incoming_b = incoming.astype(jnp.bfloat16)
    tile_rows = leaf_width // 8
    tile_count = live_count // tile_rows

    def one_tile(tile_index, merged_rows):
        row_start = tile_index * tile_rows
        diag_rows = lax.dynamic_slice_in_dim(leaf_diag, row_start, tile_rows, 0)
        out_rows = lax.dynamic_slice_in_dim(leaf_out, row_start, tile_rows, 0)
        value = jnp.dot(diag_rows, masked, preferred_element_type=jnp.float32) + jnp.dot(
            out_rows, incoming_b, preferred_element_type=jnp.float32
        )
        return lax.dynamic_update_slice_in_dim(merged_rows, value, row_start, 0)

    merged_rows = lax.fori_loop(
        0, tile_count, one_tile, jnp.zeros((leaf_width, slab_rows), jnp.float32)
    )
    updated = jnp.where(live_mask[:, None], merged_rows, slots.astype(jnp.float32)).astype(
        jnp.bfloat16
    )
    inverse = (
        jnp.zeros((leaf_width,), jnp.int32)
        .at[slot_order]
        .set(jnp.arange(leaf_width, dtype=jnp.int32))
    )
    restored = jnp.take(updated, inverse, axis=0)
    return redistribute(restored)


def solution(mesh):
    placed = (
        P(("grp", "leaf"), None),
        P(("grp", "leaf")),
        P(("grp", "leaf"), None),
        P(("grp", "leaf"), None),
        P(("grp", "leaf"), None),
        P(("grp", "leaf"), None),
        P(("grp", "leaf"), None, None),
        P(("grp", "leaf"), None, None),
        P(("grp", "leaf"), None, None),
        P(),
        P(),
        P(),
    )

    def step(basis_slab, *rest):
        devices = mesh.shape["grp"] * mesh.shape["leaf"]
        block_rows = basis_slab.shape[0] // devices
        whole_tiles = (
            block_rows % 16 == 0
            and 128 % block_rows == 0
            and mesh.shape["leaf"] % (128 // block_rows) == 0
            and basis_slab.shape[1] % (128 * MOST_CHUNKS) == 0
            and basis_slab.shape[1] % (16 * MOST_CHUNKS * mesh.shape["leaf"]) == 0
        )
        return (fused if whole_tiles else local)(basis_slab, *rest)

    return jax.shard_map(
        step, mesh=mesh, in_specs=placed, out_specs=P(("grp", "leaf"), None), check_vma=False
    )
```

```python
import functools

import jax
import jax.numpy as jnp
from jax import lax
from jax.experimental import pallas as pl
from jax.experimental.pallas import tpu as pltpu
from jax.sharding import PartitionSpec as P

MESH = pl.DeviceIdType.MESH
PERIOD = 12
COARSE = (4, 2, (-9, 3, 16, 27, 39, 53, 65, 96, 2), (8, 4, 7, 3, 2, 5, 6, 1, 0))
FINE = (8, 4, (-9, 11, 35, 51, 70, 85, 98, 121, 14), (4, 8, 7, 2, 5, 3, 0, 1, 6))
LEVELS = ((9, COARSE), (10, COARSE), (11, COARSE), (12, FINE), (13, FINE), (16, FINE))
MOST_CHUNKS = max(plan[0] for _, plan in LEVELS)


def row_dot(a, b):
    return jnp.dot(a, b, preferred_element_type=jnp.float32)


def times(matrix, rows):
    return lax.dot_general(
        rows, matrix, (((1,), (1,)), ((), ())), preferred_element_type=jnp.float32
    )


def fine_times(matrix, rows):
    high = rows.astype(jnp.bfloat16)
    low = (rows - high.astype(jnp.float32)).astype(jnp.bfloat16)
    return times(matrix, high) + times(matrix, low)


def greet(groups, leaves):
    devices = groups * leaves
    me = lax.axis_index("grp") * leaves + lax.axis_index("leaf")
    barrier = pltpu.get_barrier_semaphore()

    def body(shift, carry):
        device = lax.rem(me + shift, devices)
        pl.semaphore_signal(
            barrier,
            inc=1,
            device_id=(lax.div(device, leaves), lax.rem(device, leaves)),
            device_id_type=MESH,
        )
        return carry

    lax.fori_loop(1, devices, body, 0)
    return barrier


def census_kernel(groups, leaves, sizes, live, order, marks, level, table, send, recv):
    devices, tall, lanes = table.shape
    width = order.shape[1]
    block = width // devices
    plane = leaves * block
    per = lanes // block
    group = lax.axis_index("grp")
    seat = lax.axis_index("leaf")
    me = group * leaves + seat
    barrier = greet(groups, leaves)

    slot = lax.broadcasted_iota(jnp.int32, (1, width), 1)
    key = jnp.where(slot < live[...], order[...], -1)
    high = jnp.right_shift(key, lanes.bit_length() - 1)
    low = jnp.bitwise_and(key, lanes - 1)
    high_is = jnp.where(lax.broadcasted_iota(jnp.int32, (tall, width), 0) == high, 1.0, 0.0)
    low_is = jnp.where(lax.broadcasted_iota(jnp.int32, (lanes, width), 0) == low, 1.0, 0.0)
    table[me] = times(low_is.astype(jnp.bfloat16), high_is.astype(jnp.bfloat16))

    pl.semaphore_wait(barrier, devices - 1)

    def body(shift, carry):
        device = lax.rem(me + shift, devices)
        pltpu.make_async_remote_copy(
            src_ref=table.at[me],
            dst_ref=table.at[me],
            send_sem=send,
            recv_sem=recv,
            device_id=(lax.div(device, leaves), lax.rem(device, leaves)),
            device_id_type=MESH,
        ).start()
        return carry

    lax.fori_loop(1, devices, body, 0)
    lane = lax.broadcasted_iota(jnp.int32, (lanes, lanes), 0)
    bucket = jnp.where(
        lax.div(lane, block) == lax.broadcasted_iota(jnp.int32, (lanes, lanes), 1), 1.0, 0.0
    ).astype(jnp.bfloat16)
    lane = lax.broadcasted_iota(jnp.int32, (lanes, plane), 0)
    row = lax.broadcasted_iota(jnp.int32, (lanes, plane), 1)
    spread = jnp.where(
        lane == lax.rem(seat, per) * block + lax.rem(row, block), 1.0, 0.0
    ).astype(jnp.bfloat16)
    before = jnp.where(
        lax.broadcasted_iota(jnp.int32, (plane, plane), 0)
        < lax.broadcasted_iota(jnp.int32, (plane, plane), 1),
        1.0,
        0.0,
    ).astype(jnp.bfloat16)
    few = table.at[pl.ds(0, devices - 1)]
    pltpu.make_async_copy(few, few, recv).wait()

    owner = lax.broadcasted_iota(jnp.int32, (tall, lanes), 0) * per + lax.broadcasted_iota(
        jnp.int32, (tall, lanes), 1
    )
    inside = lax.broadcasted_iota(jnp.int32, (tall, lanes), 1) < per
    most = jnp.zeros((tall, lanes), jnp.float32)
    for target in range(groups):
        total = jnp.sum(table[target * leaves : (target + 1) * leaves], axis=0)
        counts = row_dot(total.astype(jnp.bfloat16), bucket)
        away = inside & (lax.div(owner, leaves) != target)
        most = jnp.maximum(most, jnp.where(away, counts, 0.0))
    largest = jnp.max(most)
    pick = jnp.int32(0)
    for size in sizes[:-1]:
        pick = pick + jnp.where(largest > size, 1, 0).astype(jnp.int32)
    level[0, 0] = pick

    def strip(first_leaf, device):
        rows = table[pl.ds(first_leaf, leaves)]
        at = lax.broadcasted_iota(jnp.int32, rows.shape, 1)
        return jnp.sum(jnp.where(at == lax.div(device, per), rows, 0.0), axis=1)

    strips = []
    for apart in range(groups):
        strips.append(strip(lax.rem(group - apart + groups, groups) * leaves, me))
    for apart in range(groups):
        other = lax.rem(group + apart, groups)
        strips.append(strip(group * leaves, other * leaves + seat))
    wide = row_dot(jnp.concatenate(strips, axis=0).astype(jnp.bfloat16), spread)
    leaf = lax.rem(lax.broadcasted_iota(jnp.int32, wide.shape, 0), leaves)
    here = leaf == lax.div(lax.broadcasted_iota(jnp.int32, wide.shape, 1), block)
    flags = jnp.sum(jnp.where(here, wide, 0.0).reshape(2 * groups, leaves, plane), axis=1)
    ranks = row_dot(flags.astype(jnp.bfloat16), before)
    marks[...] = jnp.where(flags > 0.5, ranks, -1.0)
    pltpu.make_async_copy(few, few, send).wait()


def fused_kernel(
    groups,
    leaves,
    plan,
    slab,
    live,
    order,
    marks,
    diag,
    gen_in,
    gen_out,
    leaf_lift,
    leaf_couple,
    leaf_spread,
    inner_lift,
    inner_couple,
    inner_spread,
    out,
    slab_here,
    pack_at,
    unpack_at,
    gone,
    there_sent,
    there_got,
    relay_in,
    arrived,
    staged,
    relay_out,
    back_sent,
    back_got,
    out_here_rows,
    diag_here,
    in_here,
    out_here,
    lifts,
    couples,
    spreads,
    lift_here,
    couple_here,
    spread_here,
    pair_sent,
    pair_got,
    select,
    diag_poles,
    in_poles,
    out_poles,
    up_sent,
    up_got,
    top,
    cross,
    down_sent,
    down_got,
    slab_sem,
    z_send,
    z_recv,
    in_send,
    in_recv,
    out_send,
    out_recv,
    tree_send,
    tree_recv,
    local_sem,
    store_sem,
    load_sem,
    pair_send,
    pair_recv,
):
    devices = groups * leaves
    chunks, width, cols = arrived.shape
    _, ahead, starts, ranks = plan
    size = there_sent.shape[2]
    block = width // devices
    plane = leaves * block
    share = groups * block
    part_cols = cols // leaves
    group = lax.axis_index("grp")
    seat = lax.axis_index("leaf")

    def seats(step):
        def body(shift, carry):
            step(lax.rem(seat + shift, leaves))
            return carry

        lax.fori_loop(1, leaves, body, 0)

    def cols_of(chunk):
        return pl.ds(pl.multiple_of(chunk * cols, cols), cols)

    def below(apart):
        return lax.rem(group - apart + groups, groups)

    def above(apart):
        return lax.rem(group + apart, groups)

    def plane_rows(which):
        return pl.ds(pl.multiple_of(which * plane, plane), plane)

    def leaf_rows(which, other):
        return pl.ds(pl.multiple_of(which * plane + other * block, block), block)

    def part_rows(index):
        return pl.ds(pl.multiple_of(index * block, block), block)

    def share_part(other, apart):
        return pl.ds(pl.multiple_of(apart * plane + other * block, block), block)

    barrier = greet(groups, leaves)

    def slab_load(chunk):
        return pltpu.make_async_copy(
            slab.at[:, cols_of(chunk)], slab_here.at[chunk], slab_sem.at[chunk]
        )

    def each(low, high, step):
        def body(index, carry):
            step(index)
            return carry

        lax.fori_loop(low, high, body, 0)

    each(0, chunks, lambda chunk: slab_load(chunk).start())

    pairs = [(diag, diag_here), (gen_in, in_here), (gen_out, out_here)]
    pairs += [(inner_lift, lifts), (inner_couple, couples), (inner_spread, spreads)]
    pairs += [(leaf_lift.at[0], lift_here), (leaf_couple.at[0], couple_here)]
    pairs += [(leaf_spread.at[0], spread_here)]
    loads = [
        pltpu.make_async_copy(source, target, load_sem.at[index])
        for index, (source, target) in enumerate(pairs)
    ]
    for load in loads:
        load.start()

    turned = marks[...].T
    row = lax.broadcasted_iota(jnp.int32, (size, plane), 0).astype(jnp.float32)
    lane = lax.broadcasted_iota(jnp.int32, (plane, size), 1).astype(jnp.float32)

    def along(role):
        return jnp.where(row == marks[role : role + 1, :], 1.0, 0.0).astype(jnp.bfloat16)

    def across(role):
        return jnp.where(lane == turned[:, role : role + 1], 1.0, 0.0).astype(jnp.bfloat16)

    for apart in range(1, groups):
        pack_at[0, apart - 1] = along(apart)
    def z_copy(source, target, way, chunk, apart, device):
        return pltpu.make_async_remote_copy(
            src_ref=source,
            dst_ref=target,
            send_sem=z_send.at[way, chunk, apart - 1],
            recv_sem=z_recv.at[way, chunk, apart - 1],
            device_id=(device, seat),
            device_id_type=MESH,
        )

    def send_there(chunk, apart):
        return z_copy(
            there_sent.at[chunk, apart - 1],
            there_got.at[chunk, apart - 1],
            0,
            chunk,
            apart,
            below(apart),
        )

    def send_back(chunk, apart):
        return z_copy(
            back_sent.at[chunk, apart - 1],
            back_got.at[chunk, apart - 1],
            1,
            chunk,
            apart,
            above(apart),
        )

    def deliver(source, chunk, apart):
        target = arrived.at[chunk, share_part(seat, apart)]
        seats(
            lambda other: pltpu.make_async_remote_copy(
                src_ref=source(other),
                dst_ref=target,
                send_sem=in_send.at[apart, chunk],
                recv_sem=in_recv.at[apart, chunk],
                device_id=(group, other),
                device_id_type=MESH,
            ).start()
        )
        pltpu.make_async_copy(source(seat), target, local_sem.at[0, apart, chunk]).start()

    def pack_in(chunk):
        slab_load(chunk).wait()

        def pack(apart):
            there_sent[chunk, apart - 1] = row_dot(
                pack_at[0, apart - 1], slab_here[chunk, plane_rows(below(apart)), :]
            ).astype(jnp.bfloat16)

        each(1, groups, pack)

    def go_in(chunk):
        each(1, groups, lambda apart: send_there(chunk, apart).start())
        deliver(lambda other: slab.at[leaf_rows(group, other), cols_of(chunk)], chunk, 0)

    def send_in(chunk):
        pack_in(chunk)
        go_in(chunk)

    def wait_bytes(buffer, chunk, rows, semaphore):
        part = buffer.at[chunk, pl.ds(0, rows)]
        pltpu.make_async_copy(part, part, semaphore).wait()

    def relay_there(chunk, apart):
        send_there(chunk, apart).wait_recv()
        relay_in[chunk, apart - 1] = row_dot(
            unpack_at[0, apart - 1], there_got[chunk, apart - 1]
        ).astype(jnp.bfloat16)
        deliver(lambda other: relay_in.at[chunk, apart - 1, part_rows(other)], chunk, apart)

    def send_out(chunk, apart):
        target = relay_out.at[chunk, apart, part_rows(seat)]
        seats(
            lambda other: pltpu.make_async_remote_copy(
                src_ref=staged.at[chunk, share_part(other, apart)],
                dst_ref=target,
                send_sem=out_send.at[apart, chunk],
                recv_sem=out_recv.at[apart, chunk],
                device_id=(group, other),
                device_id_type=MESH,
            ).start()
        )
        pltpu.make_async_copy(
            staged.at[chunk, share_part(seat, apart)], target, local_sem.at[1, apart, chunk]
        ).start()

    def wait_back(chunk, apart):
        wait_bytes(staged, chunk, (leaves - 1) * block, out_recv.at[apart, chunk])
        wait_bytes(staged, chunk, block, local_sem.at[1, apart, chunk])

    def relay_back(chunk, apart):
        wait_back(chunk, apart)
        back_sent[chunk, apart - 1] = row_dot(
            pack_at[1, apart - 1], relay_out[chunk, apart]
        ).astype(jnp.bfloat16)
        send_back(chunk, apart).start()

    def put(chunk, apart, rows):
        which = plane_rows(below(apart))
        kept = slab_here[chunk, which, :].astype(jnp.float32)
        out_here_rows[chunk, which, :] = (rows + gone[apart] * kept).astype(jnp.bfloat16)

    def stores(chunk):
        return pltpu.make_async_copy(
            out_here_rows.at[chunk], out.at[:, cols_of(chunk)], store_sem.at[chunk]
        )

    def settle(chunk, apart):
        if apart == 1:
            wait_back(chunk, 0)
            put(chunk, 0, relay_out[chunk, 0].astype(jnp.float32))

        send_back(chunk, apart).wait_recv()
        put(chunk, apart, row_dot(unpack_at[1, apart - 1], back_got[chunk, apart - 1]))
        if apart == groups - 1:
            stores(chunk).start()

    def tree_copy(source, target, chunk, stage, device):
        return pltpu.make_async_remote_copy(
            src_ref=source,
            dst_ref=target,
            send_sem=tree_send.at[stage, chunk],
            recv_sem=tree_recv.at[stage, chunk],
            device_id=device,
            device_id_type=MESH,
        )

    each(0, min(ahead, chunks), pack_in)
    pl.semaphore_wait(barrier, devices - 1)
    each(0, min(ahead, chunks), go_in)

    for apart in range(1, groups):
        unpack_at[0, apart - 1] = across(groups + apart)
        pack_at[1, apart - 1] = along(groups + apart)
        unpack_at[1, apart - 1] = across(apart)
    for apart in range(groups):
        gone[apart] = jnp.where(turned[:, apart : apart + 1] < 0.0, 1.0, 0.0)

    slot = lax.broadcasted_iota(jnp.int32, (1, width), 1)
    pole = order[...]
    apart = lax.rem(lax.div(pole, plane) - group + groups, groups)
    inner = lax.rem(pole, plane)
    moved = apart * plane + inner
    key = jnp.where(slot < live[...], moved, -1)
    part = min(256, width)
    for start in range(0, width, part):
        pole = lax.broadcasted_iota(jnp.int32, (part, width), 0) + start
        select[start : start + part, :] = jnp.where(pole == key, 1.0, 0.0).astype(jnp.bfloat16)

    for load in loads:
        load.wait()

    def fold(index, carry):
        start = pl.multiple_of(index * part, part)
        rows = pl.ds(start, part)
        chosen = select[rows, :]
        out_poles[rows, :] = row_dot(chosen, out_here[...]).astype(jnp.bfloat16)
        in_poles[rows, :] = row_dot(chosen, in_here[...])
        return carry

    lax.fori_loop(0, width // part, fold, 0)
    gather = in_poles[...].T.astype(jnp.bfloat16)

    def fold_diag(index):
        rows = pl.ds(pl.multiple_of(index * part, part), part)
        half = row_dot(select[rows, :], diag_here[...]).astype(jnp.bfloat16)
        full = lax.dot_general(
            half, select[...], (((1,), (1,)), ((), ())), preferred_element_type=jnp.float32
        )
        diag_poles[rows, :] = full.astype(jnp.bfloat16)

    def seat_rows(other):
        return pl.ds(pl.multiple_of(other * part_cols, part_cols), part_cols)

    def wait_up(chunk, semaphore):
        most = up_got.at[chunk, pl.ds(0, leaves - 1)]
        pltpu.make_async_copy(most, most, semaphore).wait()

    def wait_top(chunk, semaphore):
        most = top.at[chunk, pl.ds(0, groups - 1)]
        pltpu.make_async_copy(most, most, semaphore).wait()

    def wait_down(chunk, semaphore):
        most = down_got.at[chunk, pl.ds(0, cols - part_cols)]
        pltpu.make_async_copy(most, most, semaphore).wait()

    def node(local):
        depth = local.bit_length() - 1
        return (groups + group) * (1 << depth) + (local - (1 << depth))

    def lift_of(local):
        return lifts[node(local) - 4]

    def couple_of(local):
        return couples[node(local) - 2]

    def spread_of(local):
        return spreads[node(local) - 4]

    def pair_copy(chunk):
        return pltpu.make_async_remote_copy(
            src_ref=pair_sent.at[chunk],
            dst_ref=pair_got.at[chunk],
            send_sem=pair_send.at[chunk],
            recv_sem=pair_recv.at[chunk],
            device_id=(group, seat + 1 - 2 * lax.rem(seat, 2)),
            device_id_type=MESH,
        )

    def first(chunk):
        skeleton = jnp.zeros((gather.shape[0], cols), jnp.float32)
        for apart in range(groups):
            wait_bytes(arrived, chunk, (leaves - 1) * block, in_recv.at[apart, chunk])
            wait_bytes(arrived, chunk, block, local_sem.at[0, apart, chunk])
            low, high = apart * plane, (apart + 1) * plane
            skeleton = skeleton + row_dot(gather[:, low:high], arrived[chunk, low:high, :])
        skeleton = skeleton.T
        up_sent[chunk] = fine_times(lift_here[...], skeleton).astype(jnp.bfloat16)
        seats(
            lambda other: tree_copy(
                up_sent.at[chunk, seat_rows(other)], up_got.at[chunk, seat], chunk, 0, (group, other)
            ).start()
        )
        up_got[chunk, seat] = up_sent[chunk, seat_rows(seat), :]
        pair_sent[chunk] = fine_times(couple_here[...], skeleton).astype(jnp.bfloat16)
        pair_copy(chunk).start()

    def second(chunk):
        wait_up(chunk, tree_recv.at[0, chunk])
        skeletons = {}
        for index in range(leaves // 2):
            left = up_got[chunk, 2 * index].astype(jnp.float32)
            right = up_got[chunk, 2 * index + 1].astype(jnp.float32)
            skeletons[leaves // 2 + index] = (left + right).astype(jnp.bfloat16)
        for local in range(leaves - 1, 1, -1):
            cross[chunk, local ^ 1] = times(couple_of(local), skeletons[local])
            if local % 2 == 0:
                skeletons[local // 2] = (
                    times(lift_of(local), skeletons[local])
                    + times(lift_of(local + 1), skeletons[local + 1])
                ).astype(jnp.bfloat16)
        top[chunk, groups + group] = skeletons[1]

        def body(shift, carry):
            tree_copy(
                top.at[chunk, groups + group],
                top.at[chunk, groups + group],
                chunk,
                1,
                (lax.rem(group + shift, groups), seat),
            ).start()
            return carry

        lax.fori_loop(1, groups, body, 0)

    def third(chunk):
        wait_top(chunk, tree_recv.at[1, chunk])
        for index in range(groups - 1, 1, -1):
            top[chunk, index] = (
                times(lifts[2 * index - 4], top[chunk, 2 * index])
                + times(lifts[2 * index - 3], top[chunk, 2 * index + 1])
            ).astype(jnp.bfloat16)
        incoming = None
        for height in range(groups.bit_length() - 2, -1, -1):
            mine = lax.div(groups + group, 1 << height)
            other = mine + 1 - 2 * lax.rem(mine, 2)
            crossed = times(couples[other - 2], top[chunk, other])
            if incoming is not None:
                crossed = crossed + fine_times(spreads[mine - 4], incoming)
            incoming = crossed
        passed = {1: incoming}
        for local in range(2, leaves):
            passed[local] = (
                fine_times(spread_of(local), passed[local // 2]) + cross[chunk, local]
            )
        for index in range(leaves // 2):
            down_sent[chunk, index] = passed[leaves // 2 + index].astype(jnp.bfloat16)
        seats(
            lambda other: tree_copy(
                down_sent.at[chunk, lax.div(other, 2)],
                down_got.at[chunk, seat_rows(seat)],
                chunk,
                2,
                (group, other),
            ).start()
        )
        down_got[chunk, seat_rows(seat), :] = down_sent[chunk, lax.div(seat, 2)]

    def finish(chunk):
        wait_down(chunk, tree_recv.at[2, chunk])
        pair_copy(chunk).wait_recv()
        incoming = times(spread_here[...], down_got[chunk]) + pair_got[chunk].astype(jnp.float32)
        incoming = incoming.T.astype(jnp.bfloat16)

        def rows_done(index):
            apart = lax.rem(index + 1, groups)
            rows = plane_rows(apart)
            value = row_dot(diag_poles[rows, :], arrived[chunk]) + row_dot(
                out_poles[rows, :], incoming
            )
            staged[chunk, rows, :] = value.astype(jnp.bfloat16)
            send_out(chunk, apart)

        each(0, groups, rows_done)

    stages = (send_in, relay_there, first, second, third, finish, relay_back, settle, fold_diag)

    events = []
    for stage in range(len(stages)):
        pieces = groups - 1 if stage in (1, 6, 7) else 1
        for piece in range(pieces):
            at = starts[stage] + piece * (PERIOD // pieces)
            events.append((at % PERIOD, ranks.index(stage), stage, piece + 1, at // PERIOD))

    def period(now):
        for _, _, stage, apart, lag in sorted(events):
            chunk = now - lag
            lowest = ahead if stage == 0 else 0

            @pl.when((chunk >= lowest) & (chunk < (1 if stage == 8 else chunks)))
            def run():
                if stage == 8:
                    each(0, width // part, fold_diag)
                elif stage in (1, 6, 7):
                    stages[stage](chunk, apart)
                else:
                    stages[stage](chunk)

    each(0, max(event[-1] for event in events) + chunks, period)

    def drain(chunk):
        for apart in range(1, groups):
            send_there(chunk, apart).wait_send()
            send_back(chunk, apart).wait_send()
        for apart in range(groups):
            wait_bytes(arrived, chunk, (leaves - 1) * block, in_send.at[apart, chunk])
            wait_bytes(staged, chunk, (leaves - 1) * block, out_send.at[apart, chunk])
        wait_up(chunk, tree_send.at[0, chunk])
        wait_top(chunk, tree_send.at[1, chunk])
        wait_down(chunk, tree_send.at[2, chunk])
        pair_copy(chunk).wait_send()
        stores(chunk).wait()

    each(0, chunks, drain)


def fused(
    basis_slab,
    live_counts,
    pole_order,
    leaf_diag,
    leaf_in,
    leaf_out,
    leaf_lift,
    leaf_couple,
    leaf_spread,
    inner_lift,
    inner_couple,
    inner_spread,
):
    groups = lax.axis_size("grp")
    leaves = lax.axis_size("leaf")
    devices = groups * leaves
    width, slab_rows = basis_slab.shape
    block = width // devices
    plane = leaves * block
    rank = leaf_in.shape[1]
    vmem = pl.BlockSpec(memory_space=pltpu.VMEM)
    smem = pl.BlockSpec(memory_space=pltpu.SMEM)
    anywhere = pl.BlockSpec(memory_space=pl.ANY)
    half = jnp.bfloat16
    sizes = tuple(plane * level // LEVELS[-1][0] for level, _ in LEVELS)
    counts = live_counts.reshape(1, 1)
    lanes = 128
    marks, level = pl.pallas_call(
        functools.partial(census_kernel, groups, leaves, sizes),
        out_shape=[
            jax.ShapeDtypeStruct((2 * groups, plane), jnp.float32),
            jax.ShapeDtypeStruct((1, 1), jnp.int32),
        ],
        in_specs=[vmem] * 2,
        out_specs=[vmem, smem],
        scratch_shapes=[
            pltpu.VMEM((devices, width // lanes, lanes), jnp.float32),
            pltpu.SemaphoreType.DMA,
            pltpu.SemaphoreType.DMA,
        ],
        compiler_params=pltpu.CompilerParams(collective_id=0, has_side_effects=True),
    )(counts, pole_order)

    def main(index):
        size = sizes[index]
        plan = LEVELS[index][1]
        chunks = plan[0]
        cols = slab_rows // chunks
        away = groups - 1
        return pl.pallas_call(
            functools.partial(fused_kernel, groups, leaves, plan),
            out_shape=jax.ShapeDtypeStruct((width, slab_rows), half),
            in_specs=[anywhere] + [vmem] * 3 + [anywhere] * 9,
            out_specs=anywhere,
            scratch_shapes=[
                pltpu.VMEM((chunks, width, cols), half),
                pltpu.VMEM((2, away, size, plane), half),
                pltpu.VMEM((2, away, plane, size), half),
                pltpu.VMEM((groups, plane, 1), jnp.float32),
                pltpu.VMEM((chunks, away, size, cols), half),
                pltpu.VMEM((chunks, away, size, cols), half),
                pltpu.VMEM((chunks, away, plane, cols), half),
                pltpu.VMEM((chunks, width, cols), half),
                pltpu.VMEM((chunks, width, cols), half),
                pltpu.VMEM((chunks, groups, plane, cols), half),
                pltpu.VMEM((chunks, away, size, cols), half),
                pltpu.VMEM((chunks, away, size, cols), half),
                pltpu.VMEM((chunks, width, cols), half),
                pltpu.VMEM((width, width), half),
                pltpu.VMEM((width, rank), half),
                pltpu.VMEM((width, rank), half),
                pltpu.VMEM(inner_lift.shape, half),
                pltpu.VMEM(inner_couple.shape, half),
                pltpu.VMEM(inner_spread.shape, half),
                pltpu.VMEM((rank, rank), half),
                pltpu.VMEM((rank, rank), half),
                pltpu.VMEM((rank, rank), half),
                pltpu.VMEM((chunks, cols, rank), half),
                pltpu.VMEM((chunks, cols, rank), half),
                pltpu.VMEM((width, width), half),
                pltpu.VMEM((width, width), half),
                pltpu.VMEM((width, rank), jnp.float32),
                pltpu.VMEM((width, rank), half),
                pltpu.VMEM((chunks, cols, rank), half),
                pltpu.VMEM((chunks, leaves, cols // leaves, rank), half),
                pltpu.VMEM((chunks, 2 * groups, cols // leaves, rank), half),
                pltpu.VMEM((chunks, leaves, cols // leaves, rank), jnp.float32),
                pltpu.VMEM((chunks, leaves // 2, cols // leaves, rank), half),
                pltpu.VMEM((chunks, cols, rank), half),
                pltpu.SemaphoreType.DMA((chunks,)),
                pltpu.SemaphoreType.DMA((2, chunks, away)),
                pltpu.SemaphoreType.DMA((2, chunks, away)),
                pltpu.SemaphoreType.DMA((groups, chunks)),
                pltpu.SemaphoreType.DMA((groups, chunks)),
                pltpu.SemaphoreType.DMA((groups, chunks)),
                pltpu.SemaphoreType.DMA((groups, chunks)),
                pltpu.SemaphoreType.DMA((3, chunks)),
                pltpu.SemaphoreType.DMA((3, chunks)),
                pltpu.SemaphoreType.DMA((2, groups, chunks)),
                pltpu.SemaphoreType.DMA((chunks,)),
                pltpu.SemaphoreType.DMA((9,)),
                pltpu.SemaphoreType.DMA((chunks,)),
                pltpu.SemaphoreType.DMA((chunks,)),
            ],
            compiler_params=pltpu.CompilerParams(
                collective_id=1 + index, has_side_effects=True, vmem_limit_bytes=56 * 1024 * 1024
            ),
        )(
            basis_slab,
            counts,
            pole_order,
            marks,
            leaf_diag,
            leaf_in,
            leaf_out,
            leaf_lift,
            leaf_couple,
            leaf_spread,
            inner_lift,
            inner_couple,
            inner_spread,
        )

    branches = [functools.partial(main, index) for index in range(len(sizes))]
    return lax.switch(level[0, 0], branches)


def from_partner(block, axis, apart):
    count = lax.axis_size(axis)
    route = []
    for low in range(count):
        high = low | 1 << apart
        if high != low and high < count:
            route += [(low, high), (high, low)]
    return lax.ppermute(block, axis, route)


def transform(matrix, stacked):
    return jnp.dot(matrix.astype(jnp.float32), stacked, precision=lax.Precision.HIGHEST)


def local(
    basis_slab,
    live_counts,
    pole_order,
    leaf_diag,
    leaf_in,
    leaf_out,
    leaf_lift,
    leaf_couple,
    leaf_spread,
    inner_lift,
    inner_couple,
    inner_spread,
):
    groups = lax.axis_size("grp")
    leaves = lax.axis_size("leaf")
    devices = groups * leaves
    leaf_width = basis_slab.shape[0]
    slab_rows = basis_slab.shape[1]
    block_rows = leaf_width // devices
    levels = devices.bit_length() - 1
    leaf_bits = leaves.bit_length() - 1
    position = lax.axis_index("grp") * leaves + lax.axis_index("leaf")

    def redistribute(columns):
        arrived = lax.all_to_all(
            columns.reshape(devices, block_rows, slab_rows),
            ("grp", "leaf"),
            split_axis=0,
            concat_axis=0,
            tiled=True,
        )
        return arrived.reshape(leaf_width, slab_rows)

    def node_matrix(height, leaf_table, inner_table, offset):
        if height == 0:
            return leaf_table[0]
        own_node = jnp.right_shift(devices + position, height)
        return lax.dynamic_index_in_dim(inner_table, own_node - offset, 0, keepdims=False)

    leaf_rows = redistribute(basis_slab)
    slot_order = pole_order[0]
    live_count = live_counts[0]
    slots = jnp.take(leaf_rows, slot_order, axis=0)
    live_mask = jnp.arange(leaf_width, dtype=jnp.int32) < live_count
    masked = jnp.where(live_mask[:, None], slots, jnp.zeros_like(slots))
    skeleton = jnp.einsum("mk,mc->kc", leaf_in, masked, preferred_element_type=jnp.float32)
    crosses = []
    for height in range(leaf_bits):
        lifted = transform(node_matrix(height, leaf_lift, inner_lift, 4), skeleton)
        coupled = transform(node_matrix(height, leaf_couple, inner_couple, 2), skeleton)
        other_lift, other_cross = from_partner((lifted, coupled), "leaf", height)
        crosses.append(other_cross)
        skeleton = lifted + other_lift
    group_bits = groups.bit_length() - 1
    for height in range(leaf_bits, levels - 1):
        lifted = transform(node_matrix(height, leaf_lift, inner_lift, 4), skeleton)
        coupled = transform(node_matrix(height, leaf_couple, inner_couple, 2), skeleton)
        other_lift, other_cross = (
            from_partner(lifted.astype(jnp.bfloat16), "grp", height - leaf_bits).astype(
                lifted.dtype
            ),
            from_partner(coupled.astype(jnp.bfloat16), "grp", height - leaf_bits).astype(
                coupled.dtype
            ),
        )
        crosses.append(other_cross)
        skeleton = lifted + other_lift
    coupled = transform(node_matrix(levels - 1, leaf_couple, inner_couple, 2), skeleton)
    crosses.append(
        from_partner(coupled.astype(jnp.bfloat16), "grp", group_bits - 1).astype(coupled.dtype)
    )
    incoming = crosses[levels - 1]
    for height in range(levels - 2, -1, -1):
        incoming = (
            transform(node_matrix(height, leaf_spread, inner_spread, 4), incoming) + crosses[height]
        )
    incoming_b = incoming.astype(jnp.bfloat16)
    tile_rows = leaf_width // 8
    tile_count = live_count // tile_rows

    def one_tile(tile_index, merged_rows):
        row_start = tile_index * tile_rows
        diag_rows = lax.dynamic_slice_in_dim(leaf_diag, row_start, tile_rows, 0)
        out_rows = lax.dynamic_slice_in_dim(leaf_out, row_start, tile_rows, 0)
        value = jnp.dot(diag_rows, masked, preferred_element_type=jnp.float32) + jnp.dot(
            out_rows, incoming_b, preferred_element_type=jnp.float32
        )
        return lax.dynamic_update_slice_in_dim(merged_rows, value, row_start, 0)

    merged_rows = lax.fori_loop(
        0, tile_count, one_tile, jnp.zeros((leaf_width, slab_rows), jnp.float32)
    )
    updated = jnp.where(live_mask[:, None], merged_rows, slots.astype(jnp.float32)).astype(
        jnp.bfloat16
    )
    inverse = (
        jnp.zeros((leaf_width,), jnp.int32)
        .at[slot_order]
        .set(jnp.arange(leaf_width, dtype=jnp.int32))
    )
    restored = jnp.take(updated, inverse, axis=0)
    return redistribute(restored)


def solution(mesh):
    placed = (
        P(("grp", "leaf"), None),
        P(("grp", "leaf")),
        P(("grp", "leaf"), None),
        P(("grp", "leaf"), None),
        P(("grp", "leaf"), None),
        P(("grp", "leaf"), None),
        P(("grp", "leaf"), None, None),
        P(("grp", "leaf"), None, None),
        P(("grp", "leaf"), None, None),
        P(),
        P(),
        P(),
    )

    def step(basis_slab, *rest):
        devices = mesh.shape["grp"] * mesh.shape["leaf"]
        block_rows = basis_slab.shape[0] // devices
        whole_tiles = (
            block_rows % 16 == 0
            and 128 % block_rows == 0
            and mesh.shape["leaf"] % (128 // block_rows) == 0
            and basis_slab.shape[1] % (128 * MOST_CHUNKS) == 0
            and basis_slab.shape[1] % (16 * MOST_CHUNKS * mesh.shape["leaf"]) == 0
        )
        return (fused if whole_tiles else local)(basis_slab, *rest)

    return jax.shard_map(
        step, mesh=mesh, in_specs=placed, out_specs=P(("grp", "leaf"), None), check_vma=False
    )
```

```python
import functools

import jax
import jax.numpy as jnp
from jax import lax
from jax.experimental import pallas as pl
from jax.experimental.pallas import tpu as pltpu
from jax.sharding import PartitionSpec as P

MESH = pl.DeviceIdType.MESH
PERIOD = 12
COARSE = (4, 2, (-9, 3, 16, 27, 39, 53, 65, 96, 2), (8, 4, 7, 3, 2, 5, 6, 1, 0))
FINE = (8, 4, (-9, 11, 35, 51, 70, 85, 98, 121, 14), (4, 8, 7, 2, 5, 3, 0, 1, 6))
LEVELS = ((9, COARSE), (10, COARSE), (11, FINE), (12, FINE), (13, FINE), (16, FINE))
MOST_CHUNKS = max(plan[0] for _, plan in LEVELS)


def row_dot(a, b):
    return jnp.dot(a, b, preferred_element_type=jnp.float32)


def times(matrix, rows):
    return lax.dot_general(
        rows, matrix, (((1,), (1,)), ((), ())), preferred_element_type=jnp.float32
    )


def fine_times(matrix, rows):
    high = rows.astype(jnp.bfloat16)
    low = (rows - high.astype(jnp.float32)).astype(jnp.bfloat16)
    return times(matrix, high) + times(matrix, low)


def greet(groups, leaves):
    devices = groups * leaves
    me = lax.axis_index("grp") * leaves + lax.axis_index("leaf")
    barrier = pltpu.get_barrier_semaphore()

    def body(shift, carry):
        device = lax.rem(me + shift, devices)
        pl.semaphore_signal(
            barrier,
            inc=1,
            device_id=(lax.div(device, leaves), lax.rem(device, leaves)),
            device_id_type=MESH,
        )
        return carry

    lax.fori_loop(1, devices, body, 0)
    return barrier


def census_kernel(groups, leaves, sizes, live, order, marks, level, table, send, recv):
    devices, tall, lanes = table.shape
    width = order.shape[1]
    block = width // devices
    plane = leaves * block
    per = lanes // block
    group = lax.axis_index("grp")
    seat = lax.axis_index("leaf")
    me = group * leaves + seat
    barrier = greet(groups, leaves)

    slot = lax.broadcasted_iota(jnp.int32, (1, width), 1)
    key = jnp.where(slot < live[...], order[...], -1)
    high = jnp.right_shift(key, lanes.bit_length() - 1)
    low = jnp.bitwise_and(key, lanes - 1)
    high_is = jnp.where(lax.broadcasted_iota(jnp.int32, (tall, width), 0) == high, 1.0, 0.0)
    low_is = jnp.where(lax.broadcasted_iota(jnp.int32, (lanes, width), 0) == low, 1.0, 0.0)
    table[me] = times(low_is.astype(jnp.bfloat16), high_is.astype(jnp.bfloat16))

    pl.semaphore_wait(barrier, devices - 1)

    def body(shift, carry):
        device = lax.rem(me + shift, devices)
        pltpu.make_async_remote_copy(
            src_ref=table.at[me],
            dst_ref=table.at[me],
            send_sem=send,
            recv_sem=recv,
            device_id=(lax.div(device, leaves), lax.rem(device, leaves)),
            device_id_type=MESH,
        ).start()
        return carry

    lax.fori_loop(1, devices, body, 0)
    lane = lax.broadcasted_iota(jnp.int32, (lanes, lanes), 0)
    bucket = jnp.where(
        lax.div(lane, block) == lax.broadcasted_iota(jnp.int32, (lanes, lanes), 1), 1.0, 0.0
    ).astype(jnp.bfloat16)
    lane = lax.broadcasted_iota(jnp.int32, (lanes, plane), 0)
    row = lax.broadcasted_iota(jnp.int32, (lanes, plane), 1)
    spread = jnp.where(
        lane == lax.rem(seat, per) * block + lax.rem(row, block), 1.0, 0.0
    ).astype(jnp.bfloat16)
    before = jnp.where(
        lax.broadcasted_iota(jnp.int32, (plane, plane), 0)
        < lax.broadcasted_iota(jnp.int32, (plane, plane), 1),
        1.0,
        0.0,
    ).astype(jnp.bfloat16)
    few = table.at[pl.ds(0, devices - 1)]
    pltpu.make_async_copy(few, few, recv).wait()

    owner = lax.broadcasted_iota(jnp.int32, (tall, lanes), 0) * per + lax.broadcasted_iota(
        jnp.int32, (tall, lanes), 1
    )
    inside = lax.broadcasted_iota(jnp.int32, (tall, lanes), 1) < per
    most = jnp.zeros((tall, lanes), jnp.float32)
    for target in range(groups):
        total = jnp.sum(table[target * leaves : (target + 1) * leaves], axis=0)
        counts = row_dot(total.astype(jnp.bfloat16), bucket)
        away = inside & (lax.div(owner, leaves) != target)
        most = jnp.maximum(most, jnp.where(away, counts, 0.0))
    largest = jnp.max(most)
    pick = jnp.int32(0)
    for size in sizes[:-1]:
        pick = pick + jnp.where(largest > size, 1, 0).astype(jnp.int32)
    level[0, 0] = pick

    def strip(first_leaf, device):
        rows = table[pl.ds(first_leaf, leaves)]
        at = lax.broadcasted_iota(jnp.int32, rows.shape, 1)
        return jnp.sum(jnp.where(at == lax.div(device, per), rows, 0.0), axis=1)

    strips = []
    for apart in range(groups):
        strips.append(strip(lax.rem(group - apart + groups, groups) * leaves, me))
    for apart in range(groups):
        other = lax.rem(group + apart, groups)
        strips.append(strip(group * leaves, other * leaves + seat))
    wide = row_dot(jnp.concatenate(strips, axis=0).astype(jnp.bfloat16), spread)
    leaf = lax.rem(lax.broadcasted_iota(jnp.int32, wide.shape, 0), leaves)
    here = leaf == lax.div(lax.broadcasted_iota(jnp.int32, wide.shape, 1), block)
    flags = jnp.sum(jnp.where(here, wide, 0.0).reshape(2 * groups, leaves, plane), axis=1)
    ranks = row_dot(flags.astype(jnp.bfloat16), before)
    marks[...] = jnp.where(flags > 0.5, ranks, -1.0)
    pltpu.make_async_copy(few, few, send).wait()


def fused_kernel(
    groups,
    leaves,
    plan,
    slab,
    live,
    order,
    marks,
    diag,
    gen_in,
    gen_out,
    leaf_lift,
    leaf_couple,
    leaf_spread,
    inner_lift,
    inner_couple,
    inner_spread,
    out,
    slab_here,
    pack_at,
    unpack_at,
    gone,
    there_sent,
    there_got,
    relay_in,
    arrived,
    staged,
    relay_out,
    back_sent,
    back_got,
    out_here_rows,
    diag_here,
    in_here,
    out_here,
    lifts,
    couples,
    spreads,
    lift_here,
    couple_here,
    spread_here,
    pair_sent,
    pair_got,
    select,
    diag_poles,
    in_poles,
    out_poles,
    up_sent,
    up_got,
    top,
    cross,
    down_sent,
    down_got,
    slab_sem,
    z_send,
    z_recv,
    in_send,
    in_recv,
    out_send,
    out_recv,
    tree_send,
    tree_recv,
    local_sem,
    store_sem,
    load_sem,
    pair_send,
    pair_recv,
):
    devices = groups * leaves
    chunks, width, cols = arrived.shape
    _, ahead, starts, ranks = plan
    size = there_sent.shape[2]
    block = width // devices
    plane = leaves * block
    share = groups * block
    part_cols = cols // leaves
    group = lax.axis_index("grp")
    seat = lax.axis_index("leaf")

    def seats(step):
        def body(shift, carry):
            step(lax.rem(seat + shift, leaves))
            return carry

        lax.fori_loop(1, leaves, body, 0)

    def cols_of(chunk):
        return pl.ds(pl.multiple_of(chunk * cols, cols), cols)

    def below(apart):
        return lax.rem(group - apart + groups, groups)

    def above(apart):
        return lax.rem(group + apart, groups)

    def plane_rows(which):
        return pl.ds(pl.multiple_of(which * plane, plane), plane)

    def leaf_rows(which, other):
        return pl.ds(pl.multiple_of(which * plane + other * block, block), block)

    def part_rows(index):
        return pl.ds(pl.multiple_of(index * block, block), block)

    def share_part(other, apart):
        return pl.ds(pl.multiple_of(apart * plane + other * block, block), block)

    barrier = greet(groups, leaves)

    def slab_load(chunk):
        return pltpu.make_async_copy(
            slab.at[:, cols_of(chunk)], slab_here.at[chunk], slab_sem.at[chunk]
        )

    def each(low, high, step):
        def body(index, carry):
            step(index)
            return carry

        lax.fori_loop(low, high, body, 0)

    each(0, chunks, lambda chunk: slab_load(chunk).start())

    pairs = [(diag, diag_here), (gen_in, in_here), (gen_out, out_here)]
    pairs += [(inner_lift, lifts), (inner_couple, couples), (inner_spread, spreads)]
    pairs += [(leaf_lift.at[0], lift_here), (leaf_couple.at[0], couple_here)]
    pairs += [(leaf_spread.at[0], spread_here)]
    loads = [
        pltpu.make_async_copy(source, target, load_sem.at[index])
        for index, (source, target) in enumerate(pairs)
    ]
    for load in loads:
        load.start()

    turned = marks[...].T
    row = lax.broadcasted_iota(jnp.int32, (size, plane), 0).astype(jnp.float32)
    lane = lax.broadcasted_iota(jnp.int32, (plane, size), 1).astype(jnp.float32)

    def along(role):
        return jnp.where(row == marks[role : role + 1, :], 1.0, 0.0).astype(jnp.bfloat16)

    def across(role):
        return jnp.where(lane == turned[:, role : role + 1], 1.0, 0.0).astype(jnp.bfloat16)

    for apart in range(1, groups):
        pack_at[0, apart - 1] = along(apart)
    def z_copy(source, target, way, chunk, apart, device):
        return pltpu.make_async_remote_copy(
            src_ref=source,
            dst_ref=target,
            send_sem=z_send.at[way, chunk, apart - 1],
            recv_sem=z_recv.at[way, chunk, apart - 1],
            device_id=(device, seat),
            device_id_type=MESH,
        )

    def send_there(chunk, apart):
        return z_copy(
            there_sent.at[chunk, apart - 1],
            there_got.at[chunk, apart - 1],
            0,
            chunk,
            apart,
            below(apart),
        )

    def send_back(chunk, apart):
        return z_copy(
            back_sent.at[chunk, apart - 1],
            back_got.at[chunk, apart - 1],
            1,
            chunk,
            apart,
            above(apart),
        )

    def deliver(source, chunk, apart):
        target = arrived.at[chunk, share_part(seat, apart)]
        seats(
            lambda other: pltpu.make_async_remote_copy(
                src_ref=source(other),
                dst_ref=target,
                send_sem=in_send.at[apart, chunk],
                recv_sem=in_recv.at[apart, chunk],
                device_id=(group, other),
                device_id_type=MESH,
            ).start()
        )
        pltpu.make_async_copy(source(seat), target, local_sem.at[0, apart, chunk]).start()

    def pack_in(chunk):
        slab_load(chunk).wait()

        def pack(apart):
            there_sent[chunk, apart - 1] = row_dot(
                pack_at[0, apart - 1], slab_here[chunk, plane_rows(below(apart)), :]
            ).astype(jnp.bfloat16)

        each(1, groups, pack)

    def go_in(chunk):
        each(1, groups, lambda apart: send_there(chunk, apart).start())
        deliver(lambda other: slab.at[leaf_rows(group, other), cols_of(chunk)], chunk, 0)

    def send_in(chunk):
        pack_in(chunk)
        go_in(chunk)

    def wait_bytes(buffer, chunk, rows, semaphore):
        part = buffer.at[chunk, pl.ds(0, rows)]
        pltpu.make_async_copy(part, part, semaphore).wait()

    def relay_there(chunk, apart):
        send_there(chunk, apart).wait_recv()
        relay_in[chunk, apart - 1] = row_dot(
            unpack_at[0, apart - 1], there_got[chunk, apart - 1]
        ).astype(jnp.bfloat16)
        deliver(lambda other: relay_in.at[chunk, apart - 1, part_rows(other)], chunk, apart)

    def send_out(chunk, apart):
        target = relay_out.at[chunk, apart, part_rows(seat)]
        seats(
            lambda other: pltpu.make_async_remote_copy(
                src_ref=staged.at[chunk, share_part(other, apart)],
                dst_ref=target,
                send_sem=out_send.at[apart, chunk],
                recv_sem=out_recv.at[apart, chunk],
                device_id=(group, other),
                device_id_type=MESH,
            ).start()
        )
        pltpu.make_async_copy(
            staged.at[chunk, share_part(seat, apart)], target, local_sem.at[1, apart, chunk]
        ).start()

    def wait_back(chunk, apart):
        wait_bytes(staged, chunk, (leaves - 1) * block, out_recv.at[apart, chunk])
        wait_bytes(staged, chunk, block, local_sem.at[1, apart, chunk])

    def relay_back(chunk, apart):
        wait_back(chunk, apart)
        back_sent[chunk, apart - 1] = row_dot(
            pack_at[1, apart - 1], relay_out[chunk, apart]
        ).astype(jnp.bfloat16)
        send_back(chunk, apart).start()

    def put(chunk, apart, rows):
        which = plane_rows(below(apart))
        kept = slab_here[chunk, which, :].astype(jnp.float32)
        out_here_rows[chunk, which, :] = (rows + gone[apart] * kept).astype(jnp.bfloat16)

    def stores(chunk):
        return pltpu.make_async_copy(
            out_here_rows.at[chunk], out.at[:, cols_of(chunk)], store_sem.at[chunk]
        )

    def settle(chunk, apart):
        if apart == 1:
            wait_back(chunk, 0)
            put(chunk, 0, relay_out[chunk, 0].astype(jnp.float32))

        send_back(chunk, apart).wait_recv()
        put(chunk, apart, row_dot(unpack_at[1, apart - 1], back_got[chunk, apart - 1]))
        if apart == groups - 1:
            stores(chunk).start()

    def tree_copy(source, target, chunk, stage, device):
        return pltpu.make_async_remote_copy(
            src_ref=source,
            dst_ref=target,
            send_sem=tree_send.at[stage, chunk],
            recv_sem=tree_recv.at[stage, chunk],
            device_id=device,
            device_id_type=MESH,
        )

    each(0, min(ahead, chunks), pack_in)
    pl.semaphore_wait(barrier, devices - 1)
    each(0, min(ahead, chunks), go_in)

    for apart in range(1, groups):
        unpack_at[0, apart - 1] = across(groups + apart)
        pack_at[1, apart - 1] = along(groups + apart)
        unpack_at[1, apart - 1] = across(apart)
    for apart in range(groups):
        gone[apart] = jnp.where(turned[:, apart : apart + 1] < 0.0, 1.0, 0.0)

    slot = lax.broadcasted_iota(jnp.int32, (1, width), 1)
    pole = order[...]
    apart = lax.rem(lax.div(pole, plane) - group + groups, groups)
    inner = lax.rem(pole, plane)
    moved = apart * plane + inner
    key = jnp.where(slot < live[...], moved, -1)
    part = min(256, width)
    for start in range(0, width, part):
        pole = lax.broadcasted_iota(jnp.int32, (part, width), 0) + start
        select[start : start + part, :] = jnp.where(pole == key, 1.0, 0.0).astype(jnp.bfloat16)

    for load in loads:
        load.wait()

    def fold(index, carry):
        start = pl.multiple_of(index * part, part)
        rows = pl.ds(start, part)
        chosen = select[rows, :]
        out_poles[rows, :] = row_dot(chosen, out_here[...]).astype(jnp.bfloat16)
        in_poles[rows, :] = row_dot(chosen, in_here[...])
        return carry

    lax.fori_loop(0, width // part, fold, 0)
    gather = in_poles[...].T.astype(jnp.bfloat16)

    def fold_diag(index):
        rows = pl.ds(pl.multiple_of(index * part, part), part)
        half = row_dot(select[rows, :], diag_here[...]).astype(jnp.bfloat16)
        full = lax.dot_general(
            half, select[...], (((1,), (1,)), ((), ())), preferred_element_type=jnp.float32
        )
        diag_poles[rows, :] = full.astype(jnp.bfloat16)

    def seat_rows(other):
        return pl.ds(pl.multiple_of(other * part_cols, part_cols), part_cols)

    def wait_up(chunk, semaphore):
        most = up_got.at[chunk, pl.ds(0, leaves - 1)]
        pltpu.make_async_copy(most, most, semaphore).wait()

    def wait_top(chunk, semaphore):
        most = top.at[chunk, pl.ds(0, groups - 1)]
        pltpu.make_async_copy(most, most, semaphore).wait()

    def wait_down(chunk, semaphore):
        most = down_got.at[chunk, pl.ds(0, cols - part_cols)]
        pltpu.make_async_copy(most, most, semaphore).wait()

    def node(local):
        depth = local.bit_length() - 1
        return (groups + group) * (1 << depth) + (local - (1 << depth))

    def lift_of(local):
        return lifts[node(local) - 4]

    def couple_of(local):
        return couples[node(local) - 2]

    def spread_of(local):
        return spreads[node(local) - 4]

    def pair_copy(chunk):
        return pltpu.make_async_remote_copy(
            src_ref=pair_sent.at[chunk],
            dst_ref=pair_got.at[chunk],
            send_sem=pair_send.at[chunk],
            recv_sem=pair_recv.at[chunk],
            device_id=(group, seat + 1 - 2 * lax.rem(seat, 2)),
            device_id_type=MESH,
        )

    def first(chunk):
        skeleton = jnp.zeros((gather.shape[0], cols), jnp.float32)
        for apart in range(groups):
            wait_bytes(arrived, chunk, (leaves - 1) * block, in_recv.at[apart, chunk])
            wait_bytes(arrived, chunk, block, local_sem.at[0, apart, chunk])
            low, high = apart * plane, (apart + 1) * plane
            skeleton = skeleton + row_dot(gather[:, low:high], arrived[chunk, low:high, :])
        skeleton = skeleton.T
        up_sent[chunk] = fine_times(lift_here[...], skeleton).astype(jnp.bfloat16)
        seats(
            lambda other: tree_copy(
                up_sent.at[chunk, seat_rows(other)], up_got.at[chunk, seat], chunk, 0, (group, other)
            ).start()
        )
        up_got[chunk, seat] = up_sent[chunk, seat_rows(seat), :]
        pair_sent[chunk] = fine_times(couple_here[...], skeleton).astype(jnp.bfloat16)
        pair_copy(chunk).start()

    def second(chunk):
        wait_up(chunk, tree_recv.at[0, chunk])
        skeletons = {}
        for index in range(leaves // 2):
            left = up_got[chunk, 2 * index].astype(jnp.float32)
            right = up_got[chunk, 2 * index + 1].astype(jnp.float32)
            skeletons[leaves // 2 + index] = (left + right).astype(jnp.bfloat16)
        for local in range(leaves - 1, 1, -1):
            cross[chunk, local ^ 1] = times(couple_of(local), skeletons[local])
            if local % 2 == 0:
                skeletons[local // 2] = (
                    times(lift_of(local), skeletons[local])
                    + times(lift_of(local + 1), skeletons[local + 1])
                ).astype(jnp.bfloat16)
        top[chunk, groups + group] = skeletons[1]

        def body(shift, carry):
            tree_copy(
                top.at[chunk, groups + group],
                top.at[chunk, groups + group],
                chunk,
                1,
                (lax.rem(group + shift, groups), seat),
            ).start()
            return carry

        lax.fori_loop(1, groups, body, 0)

    def third(chunk):
        wait_top(chunk, tree_recv.at[1, chunk])
        for index in range(groups - 1, 1, -1):
            top[chunk, index] = (
                times(lifts[2 * index - 4], top[chunk, 2 * index])
                + times(lifts[2 * index - 3], top[chunk, 2 * index + 1])
            ).astype(jnp.bfloat16)
        incoming = None
        for height in range(groups.bit_length() - 2, -1, -1):
            mine = lax.div(groups + group, 1 << height)
            other = mine + 1 - 2 * lax.rem(mine, 2)
            crossed = times(couples[other - 2], top[chunk, other])
            if incoming is not None:
                crossed = crossed + fine_times(spreads[mine - 4], incoming)
            incoming = crossed
        passed = {1: incoming}
        for local in range(2, leaves):
            passed[local] = (
                fine_times(spread_of(local), passed[local // 2]) + cross[chunk, local]
            )
        for index in range(leaves // 2):
            down_sent[chunk, index] = passed[leaves // 2 + index].astype(jnp.bfloat16)
        seats(
            lambda other: tree_copy(
                down_sent.at[chunk, lax.div(other, 2)],
                down_got.at[chunk, seat_rows(seat)],
                chunk,
                2,
                (group, other),
            ).start()
        )
        down_got[chunk, seat_rows(seat), :] = down_sent[chunk, lax.div(seat, 2)]

    def finish(chunk):
        wait_down(chunk, tree_recv.at[2, chunk])
        pair_copy(chunk).wait_recv()
        incoming = times(spread_here[...], down_got[chunk]) + pair_got[chunk].astype(jnp.float32)
        incoming = incoming.T.astype(jnp.bfloat16)

        def rows_done(index):
            apart = lax.rem(index + 1, groups)
            rows = plane_rows(apart)
            value = row_dot(diag_poles[rows, :], arrived[chunk]) + row_dot(
                out_poles[rows, :], incoming
            )
            staged[chunk, rows, :] = value.astype(jnp.bfloat16)
            send_out(chunk, apart)

        each(0, groups, rows_done)

    stages = (send_in, relay_there, first, second, third, finish, relay_back, settle, fold_diag)

    events = []
    for stage in range(len(stages)):
        pieces = groups - 1 if stage in (1, 6, 7) else 1
        for piece in range(pieces):
            at = starts[stage] + piece * (PERIOD // pieces)
            events.append((at % PERIOD, ranks.index(stage), stage, piece + 1, at // PERIOD))

    def period(now):
        for _, _, stage, apart, lag in sorted(events):
            chunk = now - lag
            lowest = ahead if stage == 0 else 0

            @pl.when((chunk >= lowest) & (chunk < (1 if stage == 8 else chunks)))
            def run():
                if stage == 8:
                    each(0, width // part, fold_diag)
                elif stage in (1, 6, 7):
                    stages[stage](chunk, apart)
                else:
                    stages[stage](chunk)

    each(0, max(event[-1] for event in events) + chunks, period)

    def drain(chunk):
        for apart in range(1, groups):
            send_there(chunk, apart).wait_send()
            send_back(chunk, apart).wait_send()
        for apart in range(groups):
            wait_bytes(arrived, chunk, (leaves - 1) * block, in_send.at[apart, chunk])
            wait_bytes(staged, chunk, (leaves - 1) * block, out_send.at[apart, chunk])
        wait_up(chunk, tree_send.at[0, chunk])
        wait_top(chunk, tree_send.at[1, chunk])
        wait_down(chunk, tree_send.at[2, chunk])
        pair_copy(chunk).wait_send()
        stores(chunk).wait()

    each(0, chunks, drain)


def fused(
    basis_slab,
    live_counts,
    pole_order,
    leaf_diag,
    leaf_in,
    leaf_out,
    leaf_lift,
    leaf_couple,
    leaf_spread,
    inner_lift,
    inner_couple,
    inner_spread,
):
    groups = lax.axis_size("grp")
    leaves = lax.axis_size("leaf")
    devices = groups * leaves
    width, slab_rows = basis_slab.shape
    block = width // devices
    plane = leaves * block
    rank = leaf_in.shape[1]
    vmem = pl.BlockSpec(memory_space=pltpu.VMEM)
    smem = pl.BlockSpec(memory_space=pltpu.SMEM)
    anywhere = pl.BlockSpec(memory_space=pl.ANY)
    half = jnp.bfloat16
    sizes = tuple(plane * level // LEVELS[-1][0] for level, _ in LEVELS)
    counts = live_counts.reshape(1, 1)
    lanes = 128
    marks, level = pl.pallas_call(
        functools.partial(census_kernel, groups, leaves, sizes),
        out_shape=[
            jax.ShapeDtypeStruct((2 * groups, plane), jnp.float32),
            jax.ShapeDtypeStruct((1, 1), jnp.int32),
        ],
        in_specs=[vmem] * 2,
        out_specs=[vmem, smem],
        scratch_shapes=[
            pltpu.VMEM((devices, width // lanes, lanes), jnp.float32),
            pltpu.SemaphoreType.DMA,
            pltpu.SemaphoreType.DMA,
        ],
        compiler_params=pltpu.CompilerParams(collective_id=0, has_side_effects=True),
    )(counts, pole_order)

    def main(index):
        size = sizes[index]
        plan = LEVELS[index][1]
        chunks = plan[0]
        cols = slab_rows // chunks
        away = groups - 1
        return pl.pallas_call(
            functools.partial(fused_kernel, groups, leaves, plan),
            out_shape=jax.ShapeDtypeStruct((width, slab_rows), half),
            in_specs=[anywhere] + [vmem] * 3 + [anywhere] * 9,
            out_specs=anywhere,
            scratch_shapes=[
                pltpu.VMEM((chunks, width, cols), half),
                pltpu.VMEM((2, away, size, plane), half),
                pltpu.VMEM((2, away, plane, size), half),
                pltpu.VMEM((groups, plane, 1), jnp.float32),
                pltpu.VMEM((chunks, away, size, cols), half),
                pltpu.VMEM((chunks, away, size, cols), half),
                pltpu.VMEM((chunks, away, plane, cols), half),
                pltpu.VMEM((chunks, width, cols), half),
                pltpu.VMEM((chunks, width, cols), half),
                pltpu.VMEM((chunks, groups, plane, cols), half),
                pltpu.VMEM((chunks, away, size, cols), half),
                pltpu.VMEM((chunks, away, size, cols), half),
                pltpu.VMEM((chunks, width, cols), half),
                pltpu.VMEM((width, width), half),
                pltpu.VMEM((width, rank), half),
                pltpu.VMEM((width, rank), half),
                pltpu.VMEM(inner_lift.shape, half),
                pltpu.VMEM(inner_couple.shape, half),
                pltpu.VMEM(inner_spread.shape, half),
                pltpu.VMEM((rank, rank), half),
                pltpu.VMEM((rank, rank), half),
                pltpu.VMEM((rank, rank), half),
                pltpu.VMEM((chunks, cols, rank), half),
                pltpu.VMEM((chunks, cols, rank), half),
                pltpu.VMEM((width, width), half),
                pltpu.VMEM((width, width), half),
                pltpu.VMEM((width, rank), jnp.float32),
                pltpu.VMEM((width, rank), half),
                pltpu.VMEM((chunks, cols, rank), half),
                pltpu.VMEM((chunks, leaves, cols // leaves, rank), half),
                pltpu.VMEM((chunks, 2 * groups, cols // leaves, rank), half),
                pltpu.VMEM((chunks, leaves, cols // leaves, rank), jnp.float32),
                pltpu.VMEM((chunks, leaves // 2, cols // leaves, rank), half),
                pltpu.VMEM((chunks, cols, rank), half),
                pltpu.SemaphoreType.DMA((chunks,)),
                pltpu.SemaphoreType.DMA((2, chunks, away)),
                pltpu.SemaphoreType.DMA((2, chunks, away)),
                pltpu.SemaphoreType.DMA((groups, chunks)),
                pltpu.SemaphoreType.DMA((groups, chunks)),
                pltpu.SemaphoreType.DMA((groups, chunks)),
                pltpu.SemaphoreType.DMA((groups, chunks)),
                pltpu.SemaphoreType.DMA((3, chunks)),
                pltpu.SemaphoreType.DMA((3, chunks)),
                pltpu.SemaphoreType.DMA((2, groups, chunks)),
                pltpu.SemaphoreType.DMA((chunks,)),
                pltpu.SemaphoreType.DMA((9,)),
                pltpu.SemaphoreType.DMA((chunks,)),
                pltpu.SemaphoreType.DMA((chunks,)),
            ],
            compiler_params=pltpu.CompilerParams(
                collective_id=1 + index, has_side_effects=True, vmem_limit_bytes=56 * 1024 * 1024
            ),
        )(
            basis_slab,
            counts,
            pole_order,
            marks,
            leaf_diag,
            leaf_in,
            leaf_out,
            leaf_lift,
            leaf_couple,
            leaf_spread,
            inner_lift,
            inner_couple,
            inner_spread,
        )

    branches = [functools.partial(main, index) for index in range(len(sizes))]
    return lax.switch(level[0, 0], branches)


def from_partner(block, axis, apart):
    count = lax.axis_size(axis)
    route = []
    for low in range(count):
        high = low | 1 << apart
        if high != low and high < count:
            route += [(low, high), (high, low)]
    return lax.ppermute(block, axis, route)


def transform(matrix, stacked):
    return jnp.dot(matrix.astype(jnp.float32), stacked, precision=lax.Precision.HIGHEST)


def local(
    basis_slab,
    live_counts,
    pole_order,
    leaf_diag,
    leaf_in,
    leaf_out,
    leaf_lift,
    leaf_couple,
    leaf_spread,
    inner_lift,
    inner_couple,
    inner_spread,
):
    groups = lax.axis_size("grp")
    leaves = lax.axis_size("leaf")
    devices = groups * leaves
    leaf_width = basis_slab.shape[0]
    slab_rows = basis_slab.shape[1]
    block_rows = leaf_width // devices
    levels = devices.bit_length() - 1
    leaf_bits = leaves.bit_length() - 1
    position = lax.axis_index("grp") * leaves + lax.axis_index("leaf")

    def redistribute(columns):
        arrived = lax.all_to_all(
            columns.reshape(devices, block_rows, slab_rows),
            ("grp", "leaf"),
            split_axis=0,
            concat_axis=0,
            tiled=True,
        )
        return arrived.reshape(leaf_width, slab_rows)

    def node_matrix(height, leaf_table, inner_table, offset):
        if height == 0:
            return leaf_table[0]
        own_node = jnp.right_shift(devices + position, height)
        return lax.dynamic_index_in_dim(inner_table, own_node - offset, 0, keepdims=False)

    leaf_rows = redistribute(basis_slab)
    slot_order = pole_order[0]
    live_count = live_counts[0]
    slots = jnp.take(leaf_rows, slot_order, axis=0)
    live_mask = jnp.arange(leaf_width, dtype=jnp.int32) < live_count
    masked = jnp.where(live_mask[:, None], slots, jnp.zeros_like(slots))
    skeleton = jnp.einsum("mk,mc->kc", leaf_in, masked, preferred_element_type=jnp.float32)
    crosses = []
    for height in range(leaf_bits):
        lifted = transform(node_matrix(height, leaf_lift, inner_lift, 4), skeleton)
        coupled = transform(node_matrix(height, leaf_couple, inner_couple, 2), skeleton)
        other_lift, other_cross = from_partner((lifted, coupled), "leaf", height)
        crosses.append(other_cross)
        skeleton = lifted + other_lift
    group_bits = groups.bit_length() - 1
    for height in range(leaf_bits, levels - 1):
        lifted = transform(node_matrix(height, leaf_lift, inner_lift, 4), skeleton)
        coupled = transform(node_matrix(height, leaf_couple, inner_couple, 2), skeleton)
        other_lift, other_cross = (
            from_partner(lifted.astype(jnp.bfloat16), "grp", height - leaf_bits).astype(
                lifted.dtype
            ),
            from_partner(coupled.astype(jnp.bfloat16), "grp", height - leaf_bits).astype(
                coupled.dtype
            ),
        )
        crosses.append(other_cross)
        skeleton = lifted + other_lift
    coupled = transform(node_matrix(levels - 1, leaf_couple, inner_couple, 2), skeleton)
    crosses.append(
        from_partner(coupled.astype(jnp.bfloat16), "grp", group_bits - 1).astype(coupled.dtype)
    )
    incoming = crosses[levels - 1]
    for height in range(levels - 2, -1, -1):
        incoming = (
            transform(node_matrix(height, leaf_spread, inner_spread, 4), incoming) + crosses[height]
        )
    incoming_b = incoming.astype(jnp.bfloat16)
    tile_rows = leaf_width // 8
    tile_count = live_count // tile_rows

    def one_tile(tile_index, merged_rows):
        row_start = tile_index * tile_rows
        diag_rows = lax.dynamic_slice_in_dim(leaf_diag, row_start, tile_rows, 0)
        out_rows = lax.dynamic_slice_in_dim(leaf_out, row_start, tile_rows, 0)
        value = jnp.dot(diag_rows, masked, preferred_element_type=jnp.float32) + jnp.dot(
            out_rows, incoming_b, preferred_element_type=jnp.float32
        )
        return lax.dynamic_update_slice_in_dim(merged_rows, value, row_start, 0)

    merged_rows = lax.fori_loop(
        0, tile_count, one_tile, jnp.zeros((leaf_width, slab_rows), jnp.float32)
    )
    updated = jnp.where(live_mask[:, None], merged_rows, slots.astype(jnp.float32)).astype(
        jnp.bfloat16
    )
    inverse = (
        jnp.zeros((leaf_width,), jnp.int32)
        .at[slot_order]
        .set(jnp.arange(leaf_width, dtype=jnp.int32))
    )
    restored = jnp.take(updated, inverse, axis=0)
    return redistribute(restored)


def solution(mesh):
    placed = (
        P(("grp", "leaf"), None),
        P(("grp", "leaf")),
        P(("grp", "leaf"), None),
        P(("grp", "leaf"), None),
        P(("grp", "leaf"), None),
        P(("grp", "leaf"), None),
        P(("grp", "leaf"), None, None),
        P(("grp", "leaf"), None, None),
        P(("grp", "leaf"), None, None),
        P(),
        P(),
        P(),
    )

    def step(basis_slab, *rest):
        devices = mesh.shape["grp"] * mesh.shape["leaf"]
        block_rows = basis_slab.shape[0] // devices
        whole_tiles = (
            block_rows % 16 == 0
            and 128 % block_rows == 0
            and mesh.shape["leaf"] % (128 // block_rows) == 0
            and basis_slab.shape[1] % (128 * MOST_CHUNKS) == 0
            and basis_slab.shape[1] % (16 * MOST_CHUNKS * mesh.shape["leaf"]) == 0
        )
        return (fused if whole_tiles else local)(basis_slab, *rest)

    return jax.shard_map(
        step, mesh=mesh, in_specs=placed, out_specs=P(("grp", "leaf"), None), check_vma=False
    )
```
